256 devices in a mesh: seed: 4 (over x), chan: 16 (over z, y_lo), fsdp: 4 (over y_hi, core).
Axes of the slice: x: 4, y: 4 (y_hi: 2, y_lo: 2; y = y_hi * 2 + y_lo), z: 8, core: 2. Of those that a mesh axis runs over, the one named last changes fastest.
Arguments:
- stream: bfloat16 [256, 144, 8192], P(('seed', 'fsdp'), None, 'chan'), parts along dimension 0, may hold values from -12.5 to 9.5
- mid: bfloat16 [256, 144, 2048], P(('seed', 'fsdp'), None, 'chan'), parts along dimension 0, may hold values from 0 to 2
- conv_weight: bfloat16 [8192, 8192], P(('seed', 'fsdp'), 'chan'), parts along dimension 0, may hold values from -0.125 to 0.125
- head_weight: bfloat16 [32768, 16384], P(('seed', 'chan'), 'fsdp'), parts along dimension 0, may hold values from -0.375 to 0.375
- labels: int32 [64], replicated, may hold values from 0 to 16383
- proj_act: bfloat16 [2048, 32], replicated, may hold values from -0.125 to 0.125
- proj_err: bfloat16 [8192, 64], P('chan'), may hold values from -6 to 6
Outputs:
- grad_proj: float32 [256, 2048], P(('seed', 'fsdp'), 'chan'), parts along dimension 0
The draws below stay inside these ranges and needn't reach their ends.
There are 4 independent parts, one for each index of `seed`. The reference program is written for one: setup_inputs(seed, part) draws one part's arguments, and reference() takes and returns one part's arrays. A program takes and returns all parts, laid end to end along the dimension named above; an argument that names none is the same for every part. Nothing has to cross between parts.
All inputs are finite; a program needn't handle non-finite values.
Results may differ from the reference program's by a relative error of at most 0.01.
Values may be sent and summed in bfloat16 or wider, within the bound.
No kernel may reach another device: no remote copies, remote signals or barrier semaphores. Data moves between devices by JAX's collectives and lax.ppermute only.
A program may use at most 64 MiB of HBM per device.

```python
import jax
import jax.numpy as jnp
from jax import lax

C = 8192
MID = 2048
CLASSES = 16384
POS = 144
KA = 32
KE = 64
IMAGES = 64


def draw_stream(key, part):
    offset_key = jax.random.fold_in(key, 11)
    noise_key = jax.random.fold_in(key, 23)
    offset = -1.5 + 3.0 * jnp.clip(jax.random.normal(offset_key, (IMAGES, 1, C), jnp.float32), -3.0, 3.0)
    noise = 0.5 * jnp.clip(jax.random.normal(noise_key, (IMAGES, POS, C), jnp.float32), -4.0, 4.0)
    return (offset + noise).astype(jnp.bfloat16)


def plant(drawn, stream_key, least, top_value):
    longest = drawn.shape.index(max(drawn.shape))
    spots = []
    for shift in (0, 1):
        where = [jax.random.randint(jax.random.fold_in(stream_key, axis), (), 0, length) for axis, length in enumerate(drawn.shape)]
        where[longest] = (where[longest] + shift) % drawn.shape[longest]
        spots.append(tuple(where))
    return drawn.at[spots[0]].set(least).at[spots[1]].set(top_value)


def block_scale(stream_key, dims, shards, smallest, largest):
    gain, own = 1.0, jax.random.fold_in(stream_key, 6)
    for axis_at, parts in shards:
        steps = jnp.exp(jax.random.uniform(jax.random.fold_in(own, axis_at), (parts,), jnp.float32, smallest / len(shards), largest / len(shards)))
        gain = gain * jnp.repeat(steps, dims[axis_at] // parts).reshape([-1 if axis == axis_at else 1 for axis in range(len(dims))])
    return gain


def bell_draw(rng, dims, spread, most, shards=(), kind=jnp.bfloat16):
    result = spread * jax.random.normal(rng, dims, jnp.float32)
    if shards:
        result = result * block_scale(rng, dims, shards, -0.22, 0.18)
    return jnp.clip(result, -most, most).astype(kind)


def setup_inputs(seed: int = 0, part: int = 0) -> dict:
    key_of = jax.random.split(jax.random.key(seed), 8)
    own_keys = jax.random.split(jax.random.fold_in(key_of[7], part), 8)
    stream = draw_stream(jax.random.fold_in(jax.random.fold_in(key_of[7], part), 71), part)
    mid = jnp.clip(2.0 * jax.random.uniform(own_keys[1], (IMAGES, POS, MID), jnp.float32) ** block_scale(own_keys[1], (IMAGES, POS, MID), ((0, 4), (2, 16)), -0.2, 0.2), 0.0, 2.0).astype(jnp.bfloat16)
    conv_weight = bell_draw(own_keys[2], (MID, C), MID ** -0.5, 0.125, ((0, 4), (1, 16)))
    head_weight = bell_draw(own_keys[3], (C, CLASSES), (C // 32) ** -0.5, 0.375, ((0, 16), (1, 4)))
    labels = plant(jax.random.randint(key_of[4], (IMAGES,), 0, CLASSES), jax.random.fold_in(key_of[4], 1), 0, CLASSES - 1).astype(jnp.int32)
    proj_act = bell_draw(key_of[5], (MID, KA), MID ** -0.5, 0.125)
    proj_err = bell_draw(key_of[6], (C, KE), 1.0, 6.0, ((0, 16),))
    return dict(stream=stream, mid=mid, conv_weight=conv_weight, head_weight=head_weight, labels=labels, proj_act=proj_act, proj_err=proj_err)


def reference(stream, mid, conv_weight, head_weight, labels, proj_act, proj_err):
    images = stream.shape[0]
    mid_rows = mid.reshape(images * POS, MID)
    conv_out = jnp.dot(mid_rows, conv_weight, preferred_element_type=jnp.float32).reshape(images, POS, C)
    y_full = stream.astype(jnp.float32) + conv_out
    pooled = jnp.mean(jnp.maximum(y_full, 0.0), axis=1).astype(jnp.bfloat16)
    logits = jnp.dot(pooled, head_weight, preferred_element_type=jnp.float32)
    expo = jnp.exp(logits)
    total = jnp.sum(expo, axis=1, keepdims=True)
    onehot = (labels[:, None] == jnp.arange(CLASSES, dtype=jnp.int32)[None, :]).astype(jnp.float32)
    dlogits = (expo / total - onehot).astype(jnp.bfloat16)
    dpooled = jnp.dot(dlogits, head_weight.T, preferred_element_type=jnp.float32)
    error = jnp.where(y_full > 0.0, dpooled[:, None, :] / POS, 0.0).astype(jnp.bfloat16)
    acts_proj = jnp.dot(mid_rows, proj_act, preferred_element_type=jnp.float32).reshape(images, POS, KA)
    err_proj = jnp.dot(error.reshape(images * POS, C), proj_err, preferred_element_type=jnp.float32).reshape(images, POS, KE)
    grads = jnp.einsum("npa,npb->nab", acts_proj, err_proj, precision=lax.Precision.HIGHEST)
    return grads.reshape(images, KA * KE)
```

```python
import functools

import jax
import jax.numpy as jnp
from jax import lax
from jax.experimental import pallas as pl
from jax.experimental.pallas import tpu as pltpu
from jax.sharding import Mesh, PartitionSpec as P

CHAN = ("z", "ylo")
ROWS = ("yhi", "core", "ylo")
BF16_TOP = 3.3895313892515355e38
NT = (((1,), (1,)), ((), ()))
TN = (((0,), (0,)), ((), ()))


def conv_body(mid_ref, w_ref, stream_ref, pa_ref, pooled_ref, m_ref):
    z, two, imgs, pos, kz = mid_ref.shape
    x = jnp.concatenate(
        [mid_ref[a, b].reshape(imgs * pos, kz) for a in range(z) for b in range(two)], axis=1
    )
    acts = jnp.dot(x, pa_ref[...], preferred_element_type=jnp.float32)
    acts_hi = acts.astype(jnp.bfloat16)
    acts_lo = (acts - acts_hi.astype(jnp.float32)).astype(jnp.bfloat16)
    ka = acts.shape[1]
    acts_two = jnp.concatenate([acts_hi, acts_lo], axis=1)
    width = w_ref.shape[2]
    for h in range(two):
        y = jnp.dot(x, w_ref[h], preferred_element_type=jnp.float32)
        y = y.reshape(imgs, pos, width) + stream_ref[h].astype(jnp.float32)
        pooled_ref[0, h] = (jnp.sum(jnp.maximum(y, 0.0), axis=1) / pos).astype(jnp.bfloat16)
        mask = jnp.where(y > 0.0, 1.0, 0.0).astype(jnp.bfloat16)
        for i in range(imgs):
            both = lax.dot_general(
                acts_two[i * pos : (i + 1) * pos], mask[i], TN, preferred_element_type=jnp.float32
            )
            m_ref[i, :, h * width : (h + 1) * width] = both[:ka] + both[ka:]


def conv(mid_all, w_all, stream2, proj_act, step):
    z, two, half, pos, kz = mid_all.shape
    width = w_all.shape[2]
    depth, ka = proj_act.shape
    n = half // step
    return pl.pallas_call(
        conv_body,
        grid=(n,),
        in_specs=[
            pl.BlockSpec((z, two, step, pos, kz), lambda i: (0, 0, i, 0, 0)),
            pl.BlockSpec((two, depth, width), lambda i: (0, 0, 0), pipeline_mode=pl.Buffered(1)),
            pl.BlockSpec((two, step, pos, width), lambda i: (0, i, 0, 0)),
            pl.BlockSpec((depth, ka), lambda i: (0, 0)),
        ],
        out_specs=[
            pl.BlockSpec((1, two, step, width), lambda i: (i, 0, 0, 0)),
            pl.BlockSpec((step, ka, two * width), lambda i: (i, 0, 0)),
        ],
        out_shape=[
            jax.ShapeDtypeStruct((n, two, step, width), jnp.bfloat16),
            jax.ShapeDtypeStruct((half, ka, two * width), jnp.float32),
        ],
        compiler_params=pltpu.CompilerParams(vmem_limit_bytes=48 * 1024 * 1024),
        name="conv_pool_mask",
    )(mid_all, w_all, stream2, proj_act)


def logits_body(pooled_ref, head_ref, out_ref):
    out_ref[0] = jnp.dot(pooled_ref[...], head_ref[...], preferred_element_type=jnp.float32)


def logits_slices(pooled, head, n):
    rows, depth = pooled.shape
    share = head.shape[1] // n
    return pl.pallas_call(
        logits_body,
        grid=(n,),
        in_specs=[
            pl.BlockSpec((rows, depth), lambda i: (0, 0)),
            pl.BlockSpec((depth, share), lambda i: (0, i)),
        ],
        out_specs=pl.BlockSpec((1, rows, share), lambda i: (i, 0, 0)),
        out_shape=jax.ShapeDtypeStruct((n, rows, share), jnp.float32),
        name="logits_slices",
    )(pooled, head)


def back_body(expo_ref, head_ref, out_ref):
    depth = head_ref.shape[0]

    @pl.when(pl.program_id(0) == 0)
    def _():
        out_ref[...] = jnp.zeros_like(out_ref)

    e = expo_ref[0]
    out_ref[:, :depth] += lax.dot_general(e, head_ref[...], NT, preferred_element_type=jnp.float32)
    out_ref[:, depth:] += jnp.broadcast_to(
        jnp.sum(e.astype(jnp.float32), axis=1, keepdims=True), (out_ref.shape[0], 128)
    )


def back(expo, head):
    n, rows, share = expo.shape
    depth = head.shape[0]
    return pl.pallas_call(
        back_body,
        grid=(n,),
        in_specs=[
            pl.BlockSpec((1, rows, share), lambda i: (i, 0, 0)),
            pl.BlockSpec((depth, share), lambda i: (0, i)),
        ],
        out_specs=pl.BlockSpec((rows, depth + 128), lambda i: (0, 0)),
        out_shape=jax.ShapeDtypeStruct((rows, depth + 128), jnp.float32),
        name="back",
    )(expo, head)


def final_body(pos, m_ref, part_ref, hot_ref, pe_ref, out_ref):
    width = hot_ref.shape[3]
    imgs, ka, _ = m_ref.shape
    ke = pe_ref.shape[2]
    total = jnp.zeros((imgs, ka * ke // ka), jnp.float32)
    acc = jnp.zeros((imgs * ka, ke), jnp.float32)
    for h in range(2):
        part = sum(part_ref[a, h] for a in range(part_ref.shape[0]))
        hot = sum(hot_ref[a, h].astype(jnp.float32) for a in range(hot_ref.shape[0]))
        d = part[:, :width] / part[:, width : width + 1] - hot
        d = (d / pos).astype(jnp.bfloat16).astype(jnp.float32)
        v = (m_ref[:, :, h * width : (h + 1) * width] * d[:, None, :]).reshape(imgs * ka, width)
        v_hi = v.astype(jnp.bfloat16)
        v_lo = (v - v_hi.astype(jnp.float32)).astype(jnp.bfloat16)
        acc += jnp.dot(v_hi, pe_ref[h], preferred_element_type=jnp.float32)
        acc += jnp.dot(v_lo, pe_ref[h], preferred_element_type=jnp.float32)
    out_ref[...] = acc


def final(m, part, hot, pe, pos):
    imgs, ka, _ = m.shape
    ke = pe.shape[2]
    return pl.pallas_call(
        functools.partial(final_body, pos),
        out_shape=jax.ShapeDtypeStruct((imgs * ka, ke), jnp.float32),
        name="final",
    )(m, part, hot, pe)


def per_device(stream, mid, conv_weight, head_weight, labels, proj_act, proj_err):
    images, pos, width = stream.shape
    kz = mid.shape[2]
    half = images // 2
    parts = lax.axis_size("z") * 2
    fs = lax.axis_size("yhi") * lax.axis_size("core")
    block = head_weight.shape[1]
    me_y = lax.axis_index("ylo")
    f = lax.axis_index("yhi") * lax.axis_size("core") + lax.axis_index("core")

    mid2 = lax.all_to_all(mid.reshape(2, half, pos, kz), "ylo", 0, 0)
    mid_all = lax.all_gather(mid2, "z", axis=0)
    w_all = lax.all_gather(conv_weight, ("ylo", "yhi", "core"), axis=0)
    w_all = w_all.reshape(2, fs * conv_weight.shape[0], width)
    stream2 = lax.all_to_all(stream.reshape(2, half, pos, width), "ylo", 0, 0)
    pe = lax.all_gather(proj_err, "ylo", axis=0)

    classes = f * block + jnp.arange(block, dtype=jnp.int32)
    onehot = (labels[:, None] == classes[None, :]).astype(jnp.bfloat16)
    hot = lax.dot_general(onehot, head_weight, NT, preferred_element_type=jnp.float32)
    hot = hot.astype(jnp.bfloat16).reshape(fs, 2, half, width).reshape(2 * fs, half, width)
    hot = lax.all_to_all(hot, ROWS, 0, 0).reshape(fs, 2, half, width)

    pooled, m = conv(mid_all, w_all, stream2, proj_act, 4)
    pooled = pooled.transpose(0, 2, 1, 3).reshape(half, 2 * width)
    pooled_all = lax.all_gather(pooled, ROWS, axis=0, tiled=True)
    pooled_mine = lax.dynamic_slice_in_dim(pooled_all, me_y * width, width, 1)

    part = logits_slices(pooled_mine, head_weight, parts)
    part = lax.all_to_all(part, CHAN, 0, 0)
    expo = jnp.minimum(jnp.exp(jnp.sum(part, axis=0)), BF16_TOP).astype(jnp.bfloat16)
    expo = lax.all_gather(expo, CHAN, axis=0)

    part = back(expo, head_weight).reshape(2 * fs, half, width + 128)
    part = lax.all_to_all(part, ROWS, 0, 0).reshape(fs, 2, half, width + 128)

    grads = final(m, part, hot, pe, pos)
    grads = grads.reshape(half, parts, -1).transpose(1, 0, 2)
    grads = lax.all_to_all(grads, CHAN, 0, 0)
    grads = jnp.sum(grads.reshape(parts // 2, 2, half, -1), axis=0)
    return grads.reshape(images, -1)


def solution(mesh):
    fine = Mesh(mesh.devices.reshape(4, 8, 2, 2, 2), ("seed", "z", "ylo", "yhi", "core"))
    rows = ("seed", "yhi", "core")
    in_specs = (
        P(rows, None, CHAN),
        P(rows, None, CHAN),
        P(rows, CHAN),
        P(("seed", "z", "ylo"), ("yhi", "core")),
        P(),
        P(),
        P(CHAN, None),
    )
    return jax.shard_map(
        per_device, mesh=fine, in_specs=in_specs, out_specs=P(rows, CHAN), check_vma=False
    )
```

```python
import functools

import jax
import jax.numpy as jnp
from jax import lax
from jax.experimental import pallas as pl
from jax.experimental.pallas import tpu as pltpu
from jax.sharding import Mesh, PartitionSpec as P

CHAN = ("z", "ylo")
ROWS = ("yhi", "core", "ylo")
BF16_TOP = 3.3895313892515355e38
NT = (((1,), (1,)), ((), ()))
TN = (((0,), (0,)), ((), ()))
VM = pl.BlockSpec(memory_space=pltpu.VMEM)
LIMIT = pltpu.CompilerParams(vmem_limit_bytes=48 * 1024 * 1024)


def ring(block, nz):
    right = [(i, (i + 1) % nz) for i in range(nz)]
    left = [(i, (i - 1) % nz) for i in range(nz)]
    got = [(0, 0, block)]
    r = l = block
    for k in range(1, nz // 2):
        r = lax.ppermute(r, "z", right)
        l = lax.ppermute(l, "z", left)
        got += [(k, 0, r), (nz - k, 0, l)]
    cut = block.shape[0] // 2
    got.append((nz // 2, 0, lax.ppermute(r[:cut], "z", right)))
    got.append((nz // 2, cut, lax.ppermute(l[cut:], "z", left)))
    return got


def conv_body(nz, plan, place_ref, *refs):
    count = len(plan)
    blocks = refs[:count]
    w_ref, own_ref, other_ref, pa_ref, pooled_ref, m_ref, x_ref, acts_ref = refs[count:]
    step = pl.program_id(0)
    imgs, pos, kz = blocks[0].shape
    ka = pa_ref.shape[1]

    @pl.when(step == 0)
    def _():
        me_z = place_ref[0]
        me_y = place_ref[1]
        for ref, (sub, shift, image) in zip(blocks, plan):
            which = me_y if sub == 0 else 1 - me_y
            source = lax.rem(me_z + (nz - shift), nz)
            lane = pl.multiple_of((source * 2 + which) * kz, kz)
            flat = ref[...].reshape(ref.shape[0] * pos, kz)
            x_ref[image * pos : image * pos + flat.shape[0], pl.ds(lane, kz)] = flat
        acts = jnp.dot(x_ref[...], pa_ref[...], preferred_element_type=jnp.float32)
        hi = acts.astype(jnp.bfloat16)
        acts_ref[:, :ka] = hi
        acts_ref[:, ka:] = (acts - hi.astype(jnp.float32)).astype(jnp.bfloat16)

    def finish(stream_ref):
        y = jnp.dot(x_ref[...], w_ref[0], preferred_element_type=jnp.float32)
        width = y.shape[1]
        y = y.reshape(imgs, pos, width) + stream_ref[...].astype(jnp.float32)
        pooled = (jnp.sum(jnp.maximum(y, 0.0), axis=1) / pos).astype(jnp.bfloat16)
        for f in range(pooled_ref.shape[0]):
            pooled_ref[f, 0] = pooled
        mask = jnp.where(y > 0.0, 1.0, 0.0).astype(jnp.bfloat16)
        for i in range(imgs):
            both = lax.dot_general(
                acts_ref[i * pos : (i + 1) * pos, :], mask[i], TN, preferred_element_type=jnp.float32
            )
            m_ref[i] = both[:ka] + both[ka:]

    @pl.when(step == 0)
    def _():
        finish(own_ref.at[0])

    @pl.when(step == 1)
    def _():
        finish(other_ref)


def conv(place, got, w_all, stream2, stream_other, proj_act, nz, fs):
    plan = tuple((sub, shift, image) for sub, shift, image, _ in got)
    blocks = [b for _, _, _, b in got]
    half, pos, kz = blocks[0].shape
    _, depth, width = w_all.shape
    ka = proj_act.shape[1]

    def column(i, place):
        return jnp.where(i == 0, place[1], 1 - place[1])

    def whole(shape):
        return pl.BlockSpec(shape, lambda i, p: (0,) * len(shape), pipeline_mode=pl.Buffered(1))

    grid = pltpu.PrefetchScalarGridSpec(
        num_scalar_prefetch=1,
        grid=(2,),
        in_specs=[whole(b.shape) for b in blocks]
        + [
            pl.BlockSpec((1, depth, width), lambda i, p: (column(i, p), 0, 0)),
            pl.BlockSpec((1, half, pos, width), lambda i, p: (p[1], 0, 0, 0), pipeline_mode=pl.Buffered(1)),
            whole(stream_other.shape),
            whole(proj_act.shape),
        ],
        out_specs=[
            pl.BlockSpec((fs, 1, half, width), lambda i, p: (0, column(i, p), 0, 0)),
            pl.BlockSpec((half, ka, width), lambda i, p: (0, 0, column(i, p))),
        ],
        scratch_shapes=[
            pltpu.VMEM((half * pos, depth), jnp.bfloat16),
            pltpu.VMEM((half * pos, 2 * ka), jnp.bfloat16),
        ],
    )
    return pl.pallas_call(
        functools.partial(conv_body, nz, plan),
        grid_spec=grid,
        out_shape=[
            jax.ShapeDtypeStruct((fs, 2, half, width), jnp.bfloat16),
            jax.ShapeDtypeStruct((half, ka, 2 * width), jnp.float32),
        ],
        compiler_params=LIMIT,
        name="conv_pool_mask",
    )(place, *blocks, w_all, stream2, stream_other, proj_act)


def logits_body(pooled_ref, head_ref, out_ref):
    share = out_ref.shape[2]
    for s in range(out_ref.shape[0]):
        out_ref[s] = jnp.dot(
            pooled_ref[...], head_ref[:, s * share : (s + 1) * share], preferred_element_type=jnp.float32
        )


def logits_slices(pooled, head, n):
    rows = pooled.shape[0]
    return pl.pallas_call(
        logits_body,
        in_specs=[VM, VM],
        out_specs=VM,
        out_shape=jax.ShapeDtypeStruct((n, rows, head.shape[1] // n), jnp.float32),
        compiler_params=LIMIT,
        name="logits_slices",
    )(pooled, head)


def back_body(expo_ref, head_ref, out_ref):
    depth = head_ref.shape[0]
    e = jnp.concatenate([expo_ref[s] for s in range(expo_ref.shape[0])], axis=1)
    out_ref[:, :depth] = lax.dot_general(e, head_ref[...], NT, preferred_element_type=jnp.float32)
    total = jnp.sum(e.astype(jnp.float32), axis=1, keepdims=True)
    out_ref[:, depth:] = jnp.broadcast_to(total, (out_ref.shape[0], 128))


def back(expo, head):
    rows = expo.shape[1]
    return pl.pallas_call(
        back_body,
        in_specs=[VM, VM],
        out_specs=VM,
        out_shape=jax.ShapeDtypeStruct((rows, head.shape[0] + 128), jnp.float32),
        compiler_params=LIMIT,
        name="back",
    )(expo, head)


def final_body(pos, m_ref, part_ref, hot_ref, pe_ref, out_ref):
    width = hot_ref.shape[3]
    imgs, ka, _ = m_ref.shape
    ke = pe_ref.shape[2]
    acc = jnp.zeros((imgs * ka, ke), jnp.float32)
    for h in range(2):
        part = sum(part_ref[a, h] for a in range(part_ref.shape[0]))
        hot = sum(hot_ref[a, h].astype(jnp.float32) for a in range(hot_ref.shape[0]))
        d = part[:, :width] / part[:, width : width + 1] - hot
        d = (d / pos).astype(jnp.bfloat16).astype(jnp.float32)
        v = (m_ref[:, :, h * width : (h + 1) * width] * d[:, None, :]).reshape(imgs * ka, width)
        v_hi = v.astype(jnp.bfloat16)
        v_lo = (v - v_hi.astype(jnp.float32)).astype(jnp.bfloat16)
        acc += jnp.dot(v_hi, pe_ref[h], preferred_element_type=jnp.float32)
        acc += jnp.dot(v_lo, pe_ref[h], preferred_element_type=jnp.float32)
    out_ref[...] = acc


def final(m, part, hot, pe, pos):
    imgs, ka, _ = m.shape
    return pl.pallas_call(
        functools.partial(final_body, pos),
        in_specs=[VM] * 4,
        out_specs=VM,
        out_shape=jax.ShapeDtypeStruct((imgs * ka, pe.shape[2]), jnp.float32),
        compiler_params=LIMIT,
        name="final",
    )(m, part, hot, pe)


def per_device(stream, mid, conv_weight, head_weight, labels, proj_act, proj_err):
    images, pos, width = stream.shape
    kz = mid.shape[2]
    half = images // 2
    nz = lax.axis_size("z")
    parts = nz * 2
    fs = lax.axis_size("yhi") * lax.axis_size("core")
    block = head_weight.shape[1]
    me_y = lax.axis_index("ylo")
    f = lax.axis_index("yhi") * lax.axis_size("core") + lax.axis_index("core")
    swap = [(0, 1), (1, 0)]

    mid = mid.reshape(2, half, pos, kz)
    stream = stream.reshape(2, half, pos, width)
    mine = lax.dynamic_index_in_dim(mid, me_y, 0, keepdims=False)
    theirs = lax.dynamic_index_in_dim(mid, 1 - me_y, 0, keepdims=False)
    swapped = lax.ppermute(theirs, "ylo", swap)
    w_all = lax.all_gather(conv_weight, ("ylo", "yhi", "core"), axis=0)
    w_all = w_all.reshape(2, fs * conv_weight.shape[0], width)
    got = [(0,) + g for g in ring(mine, nz)] + [(1,) + g for g in ring(swapped, nz)]
    stream_other = lax.ppermute(
        lax.dynamic_index_in_dim(stream, 1 - me_y, 0, keepdims=False), "ylo", swap
    )

    classes = f * block + jnp.arange(block, dtype=jnp.int32)
    onehot = (labels[:, None] == classes[None, :]).astype(jnp.bfloat16)
    hot = lax.dot_general(onehot, head_weight, NT, preferred_element_type=jnp.float32)
    hot = hot.astype(jnp.bfloat16).reshape(2 * fs, half, width)
    hot = lax.all_to_all(hot, ROWS, 0, 0).reshape(fs, 2, half, width)
    pe = lax.all_gather(proj_err, "ylo", axis=0)

    *blocks, w_all, stream_other, hot, pe = lax.optimization_barrier(
        [g[3] for g in got] + [w_all, stream_other, hot, pe]
    )
    got = [g[:3] + (b,) for g, b in zip(got, blocks)]
    place = jnp.stack([lax.axis_index("z"), me_y]).astype(jnp.int32)
    pooled, m = conv(place, got, w_all, stream, stream_other, proj_act, nz, fs)

    pooled = lax.all_to_all(pooled.reshape(2 * fs, half, width), ROWS, 0, 0)
    part = logits_slices(pooled.reshape(2 * fs * half, width), head_weight, parts)
    part = lax.all_to_all(part, CHAN, 0, 0)
    expo = jnp.minimum(jnp.exp(jnp.sum(part, axis=0)), BF16_TOP).astype(jnp.bfloat16)
    expo = lax.all_to_all(jnp.broadcast_to(expo, (parts,) + expo.shape), CHAN, 0, 0)

    part = back(expo, head_weight).reshape(2 * fs, half, width + 128)
    part = lax.all_to_all(part, ROWS, 0, 0).reshape(fs, 2, half, width + 128)

    grads = final(m, part, hot, pe, pos)
    grads = grads.reshape(half, parts, -1).transpose(1, 0, 2)
    grads = lax.all_to_all(grads, CHAN, 0, 0)
    grads = jnp.sum(grads.reshape(nz, 2, half, -1), axis=0)
    return grads.reshape(images, -1)


def solution(mesh):
    fine = Mesh(mesh.devices.reshape(4, 8, 2, 2, 2), ("seed", "z", "ylo", "yhi", "core"))
    rows = ("seed", "yhi", "core")
    in_specs = (
        P(rows, None, CHAN),
        P(rows, None, CHAN),
        P(rows, CHAN),
        P(("seed", "z", "ylo"), ("yhi", "core")),
        P(),
        P(),
        P(CHAN, None),
    )
    return jax.shard_map(
        per_device, mesh=fine, in_specs=in_specs, out_specs=P(rows, CHAN), check_vma=False
    )
```

```python
import functools

import jax
import jax.numpy as jnp
from jax import lax
from jax.experimental import pallas as pl
from jax.experimental.pallas import tpu as pltpu
from jax.sharding import Mesh, PartitionSpec as P

CHAN = ("z", "ylo")
SPREAD = ("ylo", "z")
ROWS = ("yhi", "core", "ylo")
W_ORDER = ("yhi", "ylo", "core")
BF16_TOP = 3.3895313892515355e38
NT = (((1,), (1,)), ((), ()))
TN = (((0,), (0,)), ((), ()))
VM = pl.BlockSpec(memory_space=pltpu.VMEM)
HB = pl.BlockSpec(memory_space=pltpu.HBM)
LIMIT = pltpu.CompilerParams(vmem_limit_bytes=16 * 1024 * 1024)


def ring(block, nz, far):
    right = [(i, (i + 1) % nz) for i in range(nz)]
    left = [(i, (i - 1) % nz) for i in range(nz)]
    got = [(0, block)]
    r = l = block
    for k in range(1, nz // 2):
        r = lax.ppermute(r, "z", right)
        l = lax.ppermute(l, "z", left)
        got += [(k, r), (nz - k, l)]
    last = lax.ppermute(r, "z", right) if far == "right" else lax.ppermute(l, "z", left)
    return got + [(nz // 2, last)]


def conv_body(nz, plan, place_ref, *refs):
    count = len(plan)
    blocks = refs[:count]
    w_ref, own_ref, other_ref, pa_ref, hot_ref, pooled_ref, mask_ref, acts_ref = refs[count : count + 8]
    x_ref, wv_ref, sv_ref, mv_ref, x_sem, w_sem, s_sem, m_sem = refs[count + 8 :]
    imgs, pos, kz = blocks[0].shape
    cut = imgs // 2
    ka = pa_ref.shape[1]
    depth, width = wv_ref.shape[1:]
    rows_w = w_ref.shape[3]
    me_z = place_ref[0]
    me_y = place_ref[1]
    columns = (me_y, 1 - me_y)

    def copy_x(part):
        span = pl.ds(part * cut, cut)
        made = []
        for i, (ref, (sub, shift)) in enumerate(zip(blocks, plan)):
            source = lax.rem(me_z + (nz - shift), nz)
            lane = pl.multiple_of((source * 2 + columns[sub]) * kz, kz)
            made.append(
                pltpu.make_async_copy(ref.at[span], x_ref.at[span, :, pl.ds(lane, kz)], x_sem.at[part, i])
            )
        return made

    def copy_w(h):
        return [
            pltpu.make_async_copy(
                w_ref.at[hi, columns[h], core],
                wv_ref.at[h, pl.ds((hi * 2 + core) * rows_w, rows_w)],
                w_sem.at[h, hi * 2 + core],
            )
            for hi in range(2)
            for core in range(2)
        ]

    copies = [copy_w(0) + copy_x(0), copy_x(1), copy_w(1)]
    streams = [
        pltpu.make_async_copy(own_ref.at[me_y], sv_ref.at[0], s_sem.at[0]),
        pltpu.make_async_copy(other_ref, sv_ref.at[1], s_sem.at[1]),
    ]
    for c in copies[0] + [streams[0]] + copies[1] + copies[2] + [streams[1]]:
        c.start()
    pooled_ref[:, :, imgs:] = hot_ref[...]
    sends = []
    for h in range(2):
        for part in range(2):
            if h == 0:
                for c in copies[part]:
                    c.wait()
            elif part == 0:
                for c in copies[2]:
                    c.wait()
            x = x_ref[part * cut : (part + 1) * cut].reshape(cut * pos, depth)
            y = jnp.dot(x, wv_ref[h], preferred_element_type=jnp.float32)
            if h == 0:
                acts = jnp.dot(x, pa_ref[...], preferred_element_type=jnp.float32)
                hi = acts.astype(jnp.bfloat16)
                here = slice(part * cut * pos, (part + 1) * cut * pos)
                acts_ref[here, :ka] = hi
                acts_ref[here, ka:] = (acts - hi.astype(jnp.float32)).astype(jnp.bfloat16)
            if part == 0:
                streams[h].wait()
            y = y.reshape(cut, pos, width) + sv_ref[h, part * cut : (part + 1) * cut].astype(jnp.float32)
            pooled = (jnp.sum(jnp.maximum(y, 0.0), axis=1) / pos).astype(jnp.bfloat16)
            for f in range(pooled_ref.shape[0]):
                pooled_ref[f, columns[h], part * cut : (part + 1) * cut] = pooled
            mv_ref[h, part] = jnp.where(y > 0.0, 1.0, 0.0).astype(jnp.bfloat16)
            sends.append(
                pltpu.make_async_copy(
                    mv_ref.at[h, part], mask_ref.at[columns[h], pl.ds(part * cut, cut)], m_sem.at[h, part]
                )
            )
            sends[-1].start()
    for c in sends:
        c.wait()


def conv(place, got, w_all, stream2, stream_other, proj_act, hot, nz):
    plan = tuple((sub, shift) for sub, shift, _ in got)
    blocks = [b for _, _, b in got]
    half, pos, kz = blocks[0].shape
    fs, _, _, width = hot.shape
    depth, ka = proj_act.shape
    return pl.pallas_call(
        functools.partial(conv_body, nz, plan),
        in_specs=[pl.BlockSpec(memory_space=pltpu.SMEM)] + [HB] * (len(blocks) + 3) + [VM, VM],
        out_specs=[VM, HB, VM],
        out_shape=[
            jax.ShapeDtypeStruct((fs, 2, 2 * half, width), jnp.bfloat16),
            jax.ShapeDtypeStruct((2, half, pos, width), jnp.bfloat16),
            jax.ShapeDtypeStruct((half * pos, 2 * ka), jnp.bfloat16),
        ],
        scratch_shapes=[
            pltpu.VMEM((half, pos, depth), jnp.bfloat16),
            pltpu.VMEM((2, depth, width), jnp.bfloat16),
            pltpu.VMEM((2, half, pos, width), jnp.bfloat16),
            pltpu.VMEM((2, 2, half // 2, pos, width), jnp.bfloat16),
            pltpu.SemaphoreType.DMA((2, len(blocks))),
            pltpu.SemaphoreType.DMA((2, 4)),
            pltpu.SemaphoreType.DMA((2,)),
            pltpu.SemaphoreType.DMA((2, 2)),
        ],
        compiler_params=pltpu.CompilerParams(vmem_limit_bytes=32 * 1024 * 1024),
        name="conv_pool_mask",
    )(place, *[pltpu.with_memory_space_constraint(b, pltpu.HBM) for b in (*blocks, w_all, stream2, stream_other)], proj_act, hot)


def masked_body(acts_ref, mask_ref, m_ref):
    _, imgs, pos, _ = mask_ref.shape
    ka = m_ref.shape[1]
    for i in range(imgs):
        both = lax.dot_general(
            acts_ref[i * pos : (i + 1) * pos, :], mask_ref[0, i], TN, preferred_element_type=jnp.float32
        )
        m_ref[i] = both[:ka] + both[ka:]


def masked_sums(acts, mask):
    two, imgs, pos, width = mask.shape
    ka = acts.shape[1] // 2
    return pl.pallas_call(
        masked_body,
        grid=(two,),
        in_specs=[
            pl.BlockSpec(acts.shape, lambda h: (0, 0)),
            pl.BlockSpec((1, imgs, pos, width), lambda h: (h, 0, 0, 0)),
        ],
        out_specs=pl.BlockSpec((imgs, ka, width), lambda h: (0, 0, h)),
        out_shape=jax.ShapeDtypeStruct((imgs, ka, two * width), jnp.float32),
        compiler_params=LIMIT,
        name="masked_sums",
    )(acts, mask)


def logits_body(both_ref, head_ref, out_ref):
    share = out_ref.shape[2]
    some, rows, width = both_ref.shape
    pooled = both_ref[:, : rows // 2].astype(jnp.float32).reshape(some * rows // 2, width).astype(jnp.bfloat16)
    for s in range(out_ref.shape[0]):
        part = jnp.dot(pooled, head_ref[:, s * share : (s + 1) * share], preferred_element_type=jnp.float32)
        out_ref[s] = part.astype(jnp.bfloat16)


def logits_slices(both, head, n):
    some, rows, _ = both.shape
    return pl.pallas_call(
        logits_body,
        in_specs=[VM, VM],
        out_specs=VM,
        out_shape=jax.ShapeDtypeStruct((n, some * rows // 2, head.shape[1] // n), jnp.bfloat16),
        compiler_params=LIMIT,
        name="logits_slices",
    )(both, head)


def back_body(expo_ref, head_ref, out_ref, hv_ref, sem):
    depth, classes = head_ref.shape
    n, _, share = expo_ref.shape
    pieces = sem.shape[0]
    size = classes // pieces
    copies = [
        pltpu.make_async_copy(head_ref.at[:, pl.ds(p * size, size)], hv_ref.at[p], sem.at[p]) for p in range(pieces)
    ]
    for c in copies:
        c.start()
    e = jnp.concatenate([expo_ref[s] for s in range(n)], axis=1)
    total = jnp.sum(e.astype(jnp.float32), axis=1, keepdims=True)
    out_ref[:, depth:] = jnp.broadcast_to(total, (out_ref.shape[0], 128))
    acc = jnp.zeros((out_ref.shape[0], depth), jnp.float32)
    for p in range(pieces):
        copies[p].wait()
        acc += lax.dot_general(
            e[:, p * size : (p + 1) * size], hv_ref[p], NT, preferred_element_type=jnp.float32
        )
    out_ref[:, :depth] = acc


def back(expo, head):
    rows = expo.shape[1]
    depth, classes = head.shape
    pieces = 4
    return pl.pallas_call(
        back_body,
        in_specs=[VM, HB],
        out_specs=VM,
        out_shape=jax.ShapeDtypeStruct((rows, depth + 128), jnp.float32),
        scratch_shapes=[
            pltpu.VMEM((pieces, depth, classes // pieces), head.dtype),
            pltpu.SemaphoreType.DMA((pieces,)),
        ],
        compiler_params=LIMIT,
        name="back",
    )(expo, pltpu.with_memory_space_constraint(head, pltpu.HBM))


def final_body(pos, m_ref, part_ref, hot_ref, pe_ref, out_ref):
    width = hot_ref.shape[3]
    imgs, ka, _ = m_ref.shape
    ke = pe_ref.shape[2]
    acc = jnp.zeros((imgs * ka, ke), jnp.float32)
    for h in range(2):
        part = sum(part_ref[a, h] for a in range(part_ref.shape[0]))
        hot = sum(hot_ref[a, h, imgs:].astype(jnp.float32) for a in range(hot_ref.shape[0]))
        d = part[:, :width] / part[:, width : width + 1] - hot
        d = (d / pos).astype(jnp.bfloat16).astype(jnp.float32)
        v = (m_ref[:, :, h * width : (h + 1) * width] * d[:, None, :]).reshape(imgs * ka, width)
        v_hi = v.astype(jnp.bfloat16)
        v_lo = (v - v_hi.astype(jnp.float32)).astype(jnp.bfloat16)
        acc += jnp.dot(v_hi, pe_ref[h], preferred_element_type=jnp.float32)
        acc += jnp.dot(v_lo, pe_ref[h], preferred_element_type=jnp.float32)
    out_ref[...] = acc


def final(m, part, hot, pe, pos):
    imgs, ka, _ = m.shape
    return pl.pallas_call(
        functools.partial(final_body, pos),
        in_specs=[VM] * 4,
        out_specs=VM,
        out_shape=jax.ShapeDtypeStruct((imgs * ka, pe.shape[2]), jnp.float32),
        compiler_params=LIMIT,
        name="final",
    )(m, part, hot, pe)


def per_device(stream, mid, conv_weight, head_weight, labels, proj_act, proj_err):
    images, pos, width = stream.shape
    kz = mid.shape[2]
    half = images // 2
    nz = lax.axis_size("z")
    parts = nz * 2
    fs = lax.axis_size("yhi") * lax.axis_size("core")
    block = head_weight.shape[1]
    me_y = lax.axis_index("ylo")
    f = lax.axis_index("yhi") * lax.axis_size("core") + lax.axis_index("core")
    swap = [(0, 1), (1, 0)]

    mid = mid.reshape(2, half, pos, kz)
    stream = stream.reshape(2, half, pos, width)
    mine = lax.dynamic_index_in_dim(mid, me_y, 0, keepdims=False)
    theirs = lax.dynamic_index_in_dim(mid, 1 - me_y, 0, keepdims=False)
    swapped = lax.ppermute(theirs, "ylo", swap)
    w_all = lax.all_gather(conv_weight, W_ORDER, axis=0)
    w_all = w_all.reshape(2, 2, 2, *conv_weight.shape)
    got = [(0,) + g for g in ring(mine, nz, "right")] + [(1,) + g for g in ring(swapped, nz, "left")]
    stream_other = lax.ppermute(
        lax.dynamic_index_in_dim(stream, 1 - me_y, 0, keepdims=False), "ylo", swap
    )
    pe_other = lax.ppermute(proj_err, "ylo", swap)
    low = me_y == 0
    pe = jnp.stack([jnp.where(low, proj_err, pe_other), jnp.where(low, pe_other, proj_err)])

    classes = f * block + jnp.arange(block, dtype=jnp.int32)
    onehot = (labels[:, None] == classes[None, :]).astype(jnp.bfloat16)
    hot = lax.dot_general(onehot, head_weight, NT, preferred_element_type=jnp.float32)
    hot = hot.astype(jnp.bfloat16).reshape(fs, 2, half, width)

    *blocks, w_all, stream_other, pe, hot = lax.optimization_barrier(
        [g[2] for g in got] + [w_all, stream_other, pe, hot]
    )
    got = [g[:2] + (b,) for g, b in zip(got, blocks)]
    place = jnp.stack([lax.axis_index("z"), me_y]).astype(jnp.int32)
    both, mask, acts = conv(place, got, w_all, stream, stream_other, proj_act, hot, nz)

    both = lax.all_to_all(both.reshape(2 * fs, 2 * half, width), ROWS, 0, 0)
    part = lax.all_to_all(logits_slices(both, head_weight, parts), SPREAD, 0, 0)
    mask, both = lax.optimization_barrier((mask, both))
    m = masked_sums(acts, mask)
    part, m = lax.optimization_barrier((part, m))

    logits = jnp.sum(part.astype(jnp.float32), axis=0)
    expo = jnp.minimum(jnp.exp(logits), BF16_TOP).astype(jnp.bfloat16)
    expo = lax.all_to_all(jnp.broadcast_to(expo, (parts,) + expo.shape), SPREAD, 0, 0)

    part = back(expo, head_weight).reshape(2 * fs, half, width + 128)
    part = lax.all_to_all(part, ROWS, 0, 0).reshape(fs, 2, half, width + 128)

    grads = final(m, part, both.reshape(fs, 2, 2 * half, width), pe, pos)
    grads = grads.reshape(half, nz, 2, -1).transpose(2, 1, 0, 3).reshape(parts, half, -1)
    grads = lax.all_to_all(grads, SPREAD, 0, 0)
    grads = jnp.sum(grads.reshape(2, nz, half, -1), axis=1)
    return grads.reshape(images, -1)


def solution(mesh):
    fine = Mesh(mesh.devices.reshape(4, 8, 2, 2, 2), ("seed", "z", "ylo", "yhi", "core"))
    rows = ("seed", "yhi", "core")
    in_specs = (
        P(rows, None, CHAN),
        P(rows, None, CHAN),
        P(rows, CHAN),
        P(("seed", "z", "ylo"), ("yhi", "core")),
        P(),
        P(),
        P(CHAN, None),
    )
    return jax.shard_map(
        per_device, mesh=fine, in_specs=in_specs, out_specs=P(rows, CHAN), check_vma=False
    )
```

```python
import functools

import jax
import jax.numpy as jnp
from jax import lax
from jax.experimental import pallas as pl
from jax.experimental.pallas import tpu as pltpu
from jax.sharding import Mesh, PartitionSpec as P

CHAN = ("z", "ylo")
SPREAD = ("ylo", "z")
ROWS = ("yhi", "core", "ylo")
W_ORDER = ("yhi", "ylo", "core")
BF16_TOP = 3.3895313892515355e38
NT = (((1,), (1,)), ((), ()))
TN = (((0,), (0,)), ((), ()))
VM = pl.BlockSpec(memory_space=pltpu.VMEM)
HB = pl.BlockSpec(memory_space=pltpu.HBM)
LIMIT = pltpu.CompilerParams(vmem_limit_bytes=16 * 1024 * 1024)


def rings(mine, swapped, nz):
    right = [(i, (i + 1) % nz) for i in range(nz)]
    left = [(i, (i - 1) % nz) for i in range(nz)]
    got = [(0, 0, mine), (1, 0, swapped)]
    r = [mine, swapped]
    l = [mine, swapped]
    for k in range(1, nz // 2):
        for sub in range(2):
            r[sub] = lax.ppermute(r[sub], "z", right)
            l[sub] = lax.ppermute(l[sub], "z", left)
            if k < nz // 2 - 1:
                got += [(sub, k, r[sub]), (sub, nz - k, l[sub])]
    ends = [*r, *l]
    for sub in range(2):
        got += [(sub, nz // 2 - 1, ends[sub]), (sub, nz // 2 + 1, ends[2 + sub])]
    got.append((0, nz // 2, lax.ppermute(ends[0], "z", right)))
    got.append((1, nz // 2, lax.ppermute(ends[3], "z", left)))
    return got


def conv_body(nz, plan, place_ref, *refs):
    count = len(plan)
    blocks = refs[:count]
    w_ref, own_ref, other_ref, pa_ref, hot_ref, pooled_ref, mask_ref, acts_ref = refs[count : count + 8]
    x_ref, wv_ref, sv_ref, mv_ref, x_sem, w_sem, s_sem, m_sem = refs[count + 8 :]
    imgs, pos, kz = blocks[0].shape
    cut = imgs // 2
    ka = pa_ref.shape[0]
    depth, width = wv_ref.shape[1:]
    rows_w = w_ref.shape[3]
    me_z = place_ref[0]
    me_y = place_ref[1]
    columns = (me_y, 1 - me_y)

    def copy_x(part):
        span = pl.ds(part * cut, cut)
        made = []
        for i, (ref, (sub, shift)) in enumerate(zip(blocks, plan)):
            source = lax.rem(me_z + (nz - shift), nz)
            lane = pl.multiple_of((source * 2 + columns[sub]) * kz, kz)
            made.append(
                pltpu.make_async_copy(ref.at[span], x_ref.at[span, :, pl.ds(lane, kz)], x_sem.at[part, i])
            )
        return made

    def copy_w(h):
        return [
            pltpu.make_async_copy(
                w_ref.at[hi, columns[h], core],
                wv_ref.at[h, pl.ds((hi * 2 + core) * rows_w, rows_w)],
                w_sem.at[h, hi * 2 + core],
            )
            for hi in range(2)
            for core in range(2)
        ]

    copies = [copy_w(0) + copy_x(0), copy_x(1), copy_w(1)]
    streams = [
        pltpu.make_async_copy(own_ref.at[me_y], sv_ref.at[0], s_sem.at[0]),
        pltpu.make_async_copy(other_ref.at[pl.ds(0, imgs * pos)], sv_ref.at[1], s_sem.at[1]),
    ]
    for c in copies[0] + [streams[0]] + copies[1] + copies[2] + [streams[1]]:
        c.start()
    pooled_ref[:, :, imgs:] = hot_ref[...]
    sends = []
    for h in range(2):
        for part in range(2):
            if h == 0:
                for c in copies[part]:
                    c.wait()
            elif part == 0:
                for c in copies[2]:
                    c.wait()
            x = x_ref[part * cut : (part + 1) * cut].reshape(cut * pos, depth)
            y = jnp.dot(x, wv_ref[h], preferred_element_type=jnp.float32)
            if h == 0:
                acts = lax.dot_general(x, pa_ref[...], NT, preferred_element_type=jnp.float32)
                hi = acts.astype(jnp.bfloat16)
                here = slice(part * cut * pos, (part + 1) * cut * pos)
                acts_ref[here, :ka] = hi
                acts_ref[here, ka:] = (acts - hi.astype(jnp.float32)).astype(jnp.bfloat16)
            if part == 0:
                streams[h].wait()
            y = (y + sv_ref[h, part * cut * pos : (part + 1) * cut * pos].astype(jnp.float32)).reshape(cut, pos, width)
            pooled = (jnp.sum(jnp.maximum(y, 0.0), axis=1) / pos).astype(jnp.bfloat16)
            for f in range(pooled_ref.shape[0]):
                pooled_ref[f, columns[h], part * cut : (part + 1) * cut] = pooled
            mv_ref[h, part] = jnp.where(y > 0.0, 1.0, 0.0).astype(jnp.bfloat16)
            sends.append(
                pltpu.make_async_copy(
                    mv_ref.at[h, part], mask_ref.at[columns[h], pl.ds(part * cut, cut)], m_sem.at[h, part]
                )
            )
            sends[-1].start()
    for c in sends:
        c.wait()


def conv(place, got, w_all, stream2, stream_other, proj_act, hot, nz):
    plan = tuple((sub, shift) for sub, shift, _ in got)
    blocks = [b for _, _, b in got]
    half, pos, kz = blocks[0].shape
    fs, _, _, width = hot.shape
    ka, depth = proj_act.shape
    return pl.pallas_call(
        functools.partial(conv_body, nz, plan),
        in_specs=[pl.BlockSpec(memory_space=pltpu.SMEM)] + [HB] * (len(blocks) + 3) + [VM, VM],
        out_specs=[VM, HB, VM],
        out_shape=[
            jax.ShapeDtypeStruct((fs, 2, 2 * half, width), jnp.bfloat16),
            jax.ShapeDtypeStruct((2, half, pos, width), jnp.bfloat16),
            jax.ShapeDtypeStruct((half * pos, 2 * ka), jnp.bfloat16),
        ],
        scratch_shapes=[
            pltpu.VMEM((half, pos, depth), jnp.bfloat16),
            pltpu.VMEM((2, depth, width), jnp.bfloat16),
            pltpu.VMEM((2, half * pos, width), jnp.bfloat16),
            pltpu.VMEM((2, 2, half // 2, pos, width), jnp.bfloat16),
            pltpu.SemaphoreType.DMA((2, len(blocks))),
            pltpu.SemaphoreType.DMA((2, 4)),
            pltpu.SemaphoreType.DMA((2,)),
            pltpu.SemaphoreType.DMA((2, 2)),
        ],
        compiler_params=pltpu.CompilerParams(vmem_limit_bytes=32 * 1024 * 1024),
        name="conv_pool_mask",
    )(place, *[pltpu.with_memory_space_constraint(b, pltpu.HBM) for b in (*blocks, w_all, stream2, stream_other)], proj_act, hot)


def masked_body(acts_ref, mask_ref, m_ref):
    _, imgs, pos, _ = mask_ref.shape
    ka = m_ref.shape[1]
    for i in range(imgs):
        both = lax.dot_general(
            acts_ref[i * pos : (i + 1) * pos, :], mask_ref[0, i], TN, preferred_element_type=jnp.float32
        )
        m_ref[i] = both[:ka] + both[ka:]


def masked_sums(acts, mask):
    two, imgs, pos, width = mask.shape
    ka = acts.shape[1] // 2
    return pl.pallas_call(
        masked_body,
        grid=(two,),
        in_specs=[
            pl.BlockSpec(acts.shape, lambda h: (0, 0)),
            pl.BlockSpec((1, imgs, pos, width), lambda h: (h, 0, 0, 0)),
        ],
        out_specs=pl.BlockSpec((imgs, ka, width), lambda h: (0, 0, h)),
        out_shape=jax.ShapeDtypeStruct((imgs, ka, two * width), jnp.float32),
        compiler_params=LIMIT,
        name="masked_sums",
    )(acts, mask)


def logits_body(both_ref, head_ref, out_ref):
    share = out_ref.shape[2]
    some, rows, width = both_ref.shape
    pooled = both_ref[:, : rows // 2].astype(jnp.float32).reshape(some * rows // 2, width).astype(jnp.bfloat16)
    for s in range(out_ref.shape[0]):
        part = jnp.dot(pooled, head_ref[:, s * share : (s + 1) * share], preferred_element_type=jnp.float32)
        out_ref[s] = part.astype(jnp.bfloat16)


def logits_slices(both, head, n):
    some, rows, _ = both.shape
    return pl.pallas_call(
        logits_body,
        in_specs=[VM, VM],
        out_specs=VM,
        out_shape=jax.ShapeDtypeStruct((n, some * rows // 2, head.shape[1] // n), jnp.bfloat16),
        compiler_params=LIMIT,
        name="logits_slices",
    )(both, head)


def back_body(expo_ref, head_ref, out_ref, hv_ref, sem):
    depth, classes = head_ref.shape
    n, _, share = expo_ref.shape
    pieces = sem.shape[0]
    size = classes // pieces
    copies = [
        pltpu.make_async_copy(head_ref.at[:, pl.ds(p * size, size)], hv_ref.at[p], sem.at[p]) for p in range(pieces)
    ]
    for c in copies:
        c.start()
    e = jnp.concatenate([expo_ref[s] for s in range(n)], axis=1)
    total = jnp.sum(e.astype(jnp.float32), axis=1, keepdims=True)
    out_ref[:, depth:] = jnp.broadcast_to(total, (out_ref.shape[0], 128))
    acc = jnp.zeros((out_ref.shape[0], depth), jnp.float32)
    for p in range(pieces):
        copies[p].wait()
        acc += lax.dot_general(
            e[:, p * size : (p + 1) * size], hv_ref[p], NT, preferred_element_type=jnp.float32
        )
    out_ref[:, :depth] = acc


def back(expo, head):
    rows = expo.shape[1]
    depth, classes = head.shape
    pieces = 4
    return pl.pallas_call(
        back_body,
        in_specs=[VM, HB],
        out_specs=VM,
        out_shape=jax.ShapeDtypeStruct((rows, depth + 128), jnp.float32),
        scratch_shapes=[
            pltpu.VMEM((pieces, depth, classes // pieces), head.dtype),
            pltpu.SemaphoreType.DMA((pieces,)),
        ],
        compiler_params=LIMIT,
        name="back",
    )(expo, pltpu.with_memory_space_constraint(head, pltpu.HBM))


def final_body(pos, place_ref, m_ref, part_ref, hot_ref, own_ref, other_ref, out_ref):
    width = hot_ref.shape[3]
    imgs, ka, _ = m_ref.shape
    acc = jnp.zeros(out_ref.shape, jnp.float32)
    for k, pe_ref in enumerate((own_ref, other_ref)):
        h = place_ref[1] if k == 0 else 1 - place_ref[1]
        part = sum(part_ref[a, h] for a in range(part_ref.shape[0]))
        hot = sum(hot_ref[a, h].astype(jnp.float32)[imgs:] for a in range(hot_ref.shape[0]))
        d = part[:, :width] / part[:, width : width + 1] - hot
        d = (d / pos).astype(jnp.bfloat16).astype(jnp.float32)
        lane = pl.multiple_of(h * width, width)
        v = (m_ref[:, :, pl.ds(lane, width)] * d[:, None, :]).reshape(imgs * ka, width)
        v_hi = v.astype(jnp.bfloat16)
        v_lo = (v - v_hi.astype(jnp.float32)).astype(jnp.bfloat16)
        acc += lax.dot_general(v_hi, pe_ref[...], NT, preferred_element_type=jnp.float32)
        acc += lax.dot_general(v_lo, pe_ref[...], NT, preferred_element_type=jnp.float32)
    out_ref[...] = acc


def final(place, m, part, hot, pe_own, pe_other, pos):
    imgs, ka, _ = m.shape
    return pl.pallas_call(
        functools.partial(final_body, pos),
        in_specs=[pl.BlockSpec(memory_space=pltpu.SMEM)] + [VM] * 5,
        out_specs=VM,
        out_shape=jax.ShapeDtypeStruct((imgs * ka, pe_own.shape[0]), jnp.float32),
        compiler_params=LIMIT,
        name="final",
    )(place, m, part, hot, pe_own, pe_other)


def per_device(stream, mid, conv_weight, head_weight, labels, proj_act, proj_err):
    images, pos, width = stream.shape
    kz = mid.shape[2]
    half = images // 2
    nz = lax.axis_size("z")
    parts = nz * 2
    fs = lax.axis_size("yhi") * lax.axis_size("core")
    block = head_weight.shape[1]
    me_y = lax.axis_index("ylo")
    f = lax.axis_index("yhi") * lax.axis_size("core") + lax.axis_index("core")
    swap = [(0, 1), (1, 0)]

    mid = mid.reshape(2, half, pos, kz)
    stream = stream.reshape(2, half, pos, width)
    mine = lax.dynamic_index_in_dim(mid, me_y, 0, keepdims=False)
    theirs = lax.dynamic_index_in_dim(mid, 1 - me_y, 0, keepdims=False)
    swapped = lax.ppermute(theirs, "ylo", swap)
    pe_own = proj_err.T
    sent = lax.dynamic_index_in_dim(stream, 1 - me_y, 0, keepdims=False).reshape(half * pos, width)
    stream_other = lax.ppermute(jnp.concatenate([sent, pe_own], axis=0), "ylo", swap)
    w_all = lax.all_gather(conv_weight, W_ORDER, axis=0)
    got = rings(mine, swapped, nz)

    classes = f * block + jnp.arange(block, dtype=jnp.int32)
    onehot = (labels[:, None] == classes[None, :]).astype(jnp.bfloat16)
    hot = lax.dot_general(onehot, head_weight, NT, preferred_element_type=jnp.float32)
    hot = hot.astype(jnp.bfloat16).reshape(fs, 2, half, width)

    *blocks, w_all, stream_other, hot = lax.optimization_barrier(
        [g[2] for g in got] + [w_all, stream_other, hot]
    )
    got = [g[:2] + (b,) for g, b in zip(got, blocks)]
    place = jnp.stack([lax.axis_index("z"), me_y]).astype(jnp.int32)
    both, mask, acts = conv(
        place, got, w_all.reshape(2, 2, 2, *conv_weight.shape),
        stream.reshape(2, half * pos, width), stream_other, proj_act.T, hot, nz,
    )

    both = lax.all_to_all(both.reshape(2 * fs, 2 * half, width), ROWS, 0, 0)
    part = lax.all_to_all(logits_slices(both, head_weight, parts), SPREAD, 0, 0)
    mask, both = lax.optimization_barrier((mask, both))
    m = masked_sums(acts, mask)
    pe_other = stream_other[half * pos :]
    part, m, pe_other = lax.optimization_barrier((part, m, pe_other))

    logits = jnp.sum(part.astype(jnp.float32), axis=0)
    expo = jnp.minimum(jnp.exp(logits), BF16_TOP).astype(jnp.bfloat16)
    expo = lax.all_to_all(jnp.broadcast_to(expo, (parts,) + expo.shape), SPREAD, 0, 0)

    part = back(expo, head_weight).reshape(2 * fs, half, width + 128)
    part = lax.all_to_all(part, ROWS, 0, 0).reshape(fs, 2, half, width + 128)

    grads = final(place, m, part, both.reshape(fs, 2, 2 * half, width), pe_own, pe_other, pos)
    grads = grads.reshape(half, nz, 2, -1).transpose(2, 1, 0, 3).reshape(parts, half, -1)
    grads = lax.all_to_all(grads, SPREAD, 0, 0)
    grads = jnp.sum(grads.reshape(2, nz, half, -1), axis=1)
    return grads.reshape(images, -1)


def solution(mesh):
    fine = Mesh(mesh.devices.reshape(4, 8, 2, 2, 2), ("seed", "z", "ylo", "yhi", "core"))
    rows = ("seed", "yhi", "core")
    in_specs = (
        P(rows, None, CHAN),
        P(rows, None, CHAN),
        P(rows, CHAN),
        P(("seed", "z", "ylo"), ("yhi", "core")),
        P(),
        P(),
        P(CHAN, None),
    )
    return jax.shard_map(
        per_device, mesh=fine, in_specs=in_specs, out_specs=P(rows, CHAN), check_vma=False
    )
```

```python
import functools

import jax
import jax.numpy as jnp
from jax import lax
from jax.experimental import pallas as pl
from jax.experimental.pallas import tpu as pltpu
from jax.sharding import Mesh, PartitionSpec as P

CHAN = ("z", "ylo")
SPREAD = ("ylo", "z")
ROWS = ("yhi", "core", "ylo")
BF16_TOP = 3.3895313892515355e38
NT = (((1,), (1,)), ((), ()))
TN = (((0,), (0,)), ((), ()))
VM = pl.BlockSpec(memory_space=pltpu.VMEM)
HB = pl.BlockSpec(memory_space=pltpu.HBM)
LIMIT = pltpu.CompilerParams(vmem_limit_bytes=16 * 1024 * 1024)


def pass_weight(w):
    swap = [(0, 1), (1, 0)]
    across = [(i, 3 - i) for i in range(4)]
    low = lax.ppermute(w, "ylo", swap)
    high = lax.ppermute(w, ("ylo", "yhi"), across)
    far = lax.ppermute(low, ("ylo", "yhi"), across)
    return [b for v in (w, far, low, high) for b in (v, lax.ppermute(v, "core", swap))]


def rings(mine, swapped, nz):
    right = [(i, (i + 1) % nz) for i in range(nz)]
    left = [(i, (i - 1) % nz) for i in range(nz)]
    r = [lax.ppermute(mine, "z", right), None]
    l = [lax.ppermute(mine, "z", left), None]
    r[0], l[0], swapped = lax.optimization_barrier((r[0], l[0], swapped))
    got = [(0, 0, mine), (1, 0, swapped), (0, 1, r[0]), (0, nz - 1, l[0])]
    r[1] = l[1] = swapped
    for k in range(1, nz // 2):
        for sub in range(2):
            step = k if sub else k + 1
            if step < nz // 2:
                r[sub] = lax.ppermute(r[sub], "z", right)
                l[sub] = lax.ppermute(l[sub], "z", left)
                got += [(sub, step, r[sub]), (sub, nz - step, l[sub])]
    got.append((0, nz // 2, lax.ppermute(r[0], "z", right)))
    got.append((1, nz // 2, lax.ppermute(l[1], "z", left)))
    return got


def conv_body(nz, plan, place_ref, *refs):
    count = len(plan)
    blocks = refs[:count]
    w_refs = refs[count : count + 8]
    own_ref, other_ref, pa_ref, hot_ref, pooled_ref, mask_ref, acts_ref = refs[count + 8 : count + 15]
    x_ref, wv_ref, sv_ref, mv_ref, x_sem, w_sem, s_sem, m_sem = refs[count + 15 :]
    imgs, pos, kz = blocks[0].shape
    cut = imgs // 2
    ka = pa_ref.shape[0]
    depth, width = wv_ref.shape[1:]
    rows_w = w_refs[0].shape[0]
    me_z = place_ref[0]
    me_y = place_ref[1]
    me_hi = place_ref[2]
    me_core = place_ref[3]
    columns = (me_y, 1 - me_y)

    def copy_x(part):
        span = pl.ds(part * cut, cut)
        made = []
        for i, (ref, (sub, shift)) in enumerate(zip(blocks, plan)):
            source = lax.rem(me_z + (nz - shift), nz)
            lane = pl.multiple_of((source * 2 + columns[sub]) * kz, kz)
            made.append(
                pltpu.make_async_copy(ref.at[span], x_ref.at[span, :, pl.ds(lane, kz)], x_sem.at[part, i])
            )
        return made

    def copy_w(h):
        made = []
        for i in range(4):
            hi = me_hi if i < 2 else 1 - me_hi
            core = me_core if i % 2 == 0 else 1 - me_core
            row = pl.multiple_of((hi * 2 + core) * rows_w, rows_w)
            made.append(pltpu.make_async_copy(w_refs[4 * h + i], wv_ref.at[h, pl.ds(row, rows_w)], w_sem.at[h, i]))
        return made

    copies = [copy_w(0) + copy_x(0), copy_x(1), copy_w(1)]
    streams = [
        pltpu.make_async_copy(own_ref.at[me_y], sv_ref.at[0], s_sem.at[0]),
        pltpu.make_async_copy(other_ref.at[pl.ds(0, imgs * pos)], sv_ref.at[1], s_sem.at[1]),
    ]
    for c in copies[0] + [streams[0]] + copies[1] + copies[2] + [streams[1]]:
        c.start()
    pooled_ref[:, :, imgs:] = hot_ref[...]
    sends = []
    for h in range(2):
        for part in range(2):
            if h == 0:
                for c in copies[part]:
                    c.wait()
            elif part == 0:
                for c in copies[2]:
                    c.wait()
            x = x_ref[part * cut : (part + 1) * cut].reshape(cut * pos, depth)
            y = jnp.dot(x, wv_ref[h], preferred_element_type=jnp.float32)
            if h == 0:
                acts = lax.dot_general(x, pa_ref[...], NT, preferred_element_type=jnp.float32)
                hi = acts.astype(jnp.bfloat16)
                here = slice(part * cut * pos, (part + 1) * cut * pos)
                acts_ref[here, :ka] = hi
                acts_ref[here, ka:] = (acts - hi.astype(jnp.float32)).astype(jnp.bfloat16)
            if part == 0:
                streams[h].wait()
            y = (y + sv_ref[h, part * cut * pos : (part + 1) * cut * pos].astype(jnp.float32)).reshape(cut, pos, width)
            pooled = (jnp.sum(jnp.maximum(y, 0.0), axis=1) / pos).astype(jnp.bfloat16)
            for f in range(pooled_ref.shape[0]):
                pooled_ref[f, columns[h], part * cut : (part + 1) * cut] = pooled
            mv_ref[h, part] = jnp.where(y > 0.0, 1.0, 0.0).astype(jnp.bfloat16)
            sends.append(
                pltpu.make_async_copy(
                    mv_ref.at[h, part], mask_ref.at[columns[h], pl.ds(part * cut, cut)], m_sem.at[h, part]
                )
            )
            sends[-1].start()
    for c in sends:
        c.wait()


def conv(place, got, weights, stream2, stream_other, proj_act, hot, nz):
    plan = tuple((sub, shift) for sub, shift, _ in got)
    blocks = [b for _, _, b in got]
    half, pos, kz = blocks[0].shape
    fs, _, _, width = hot.shape
    ka, depth = proj_act.shape
    return pl.pallas_call(
        functools.partial(conv_body, nz, plan),
        in_specs=[pl.BlockSpec(memory_space=pltpu.SMEM)] + [HB] * (len(blocks) + 10) + [VM, VM],
        out_specs=[VM, HB, VM],
        out_shape=[
            jax.ShapeDtypeStruct((fs, 2, 2 * half, width), jnp.bfloat16),
            jax.ShapeDtypeStruct((2, half, pos, width), jnp.bfloat16),
            jax.ShapeDtypeStruct((half * pos, 2 * ka), jnp.bfloat16),
        ],
        scratch_shapes=[
            pltpu.VMEM((half, pos, depth), jnp.bfloat16),
            pltpu.VMEM((2, depth, width), jnp.bfloat16),
            pltpu.VMEM((2, half * pos, width), jnp.bfloat16),
            pltpu.VMEM((2, 2, half // 2, pos, width), jnp.bfloat16),
            pltpu.SemaphoreType.DMA((2, len(blocks))),
            pltpu.SemaphoreType.DMA((2, 4)),
            pltpu.SemaphoreType.DMA((2,)),
            pltpu.SemaphoreType.DMA((2, 2)),
        ],
        compiler_params=pltpu.CompilerParams(vmem_limit_bytes=32 * 1024 * 1024),
        name="conv_pool_mask",
    )(place, *[pltpu.with_memory_space_constraint(b, pltpu.HBM) for b in (*blocks, *weights, stream2, stream_other)], proj_act, hot)


def masked_body(acts_ref, mask_ref, m_ref):
    _, imgs, pos, _ = mask_ref.shape
    ka = m_ref.shape[1]
    for i in range(imgs):
        both = lax.dot_general(
            acts_ref[i * pos : (i + 1) * pos, :], mask_ref[0, i], TN, preferred_element_type=jnp.float32
        )
        m_ref[i] = both[:ka] + both[ka:]


def masked_sums(acts, mask):
    two, imgs, pos, width = mask.shape
    ka = acts.shape[1] // 2
    return pl.pallas_call(
        masked_body,
        grid=(two,),
        in_specs=[
            pl.BlockSpec(acts.shape, lambda h: (0, 0)),
            pl.BlockSpec((1, imgs, pos, width), lambda h: (h, 0, 0, 0)),
        ],
        out_specs=pl.BlockSpec((imgs, ka, width), lambda h: (0, 0, h)),
        out_shape=jax.ShapeDtypeStruct((imgs, ka, two * width), jnp.float32),
        compiler_params=LIMIT,
        name="masked_sums",
    )(acts, mask)


def logits_body(both_ref, head_ref, out_ref):
    share = out_ref.shape[2]
    some, rows, width = both_ref.shape
    pooled = both_ref[:, : rows // 2].astype(jnp.float32).reshape(some * rows // 2, width).astype(jnp.bfloat16)
    for s in range(out_ref.shape[0]):
        part = jnp.dot(pooled, head_ref[:, s * share : (s + 1) * share], preferred_element_type=jnp.float32)
        out_ref[s] = part.astype(jnp.bfloat16)


def logits_slices(both, head, n):
    some, rows, _ = both.shape
    return pl.pallas_call(
        logits_body,
        in_specs=[VM, VM],
        out_specs=VM,
        out_shape=jax.ShapeDtypeStruct((n, some * rows // 2, head.shape[1] // n), jnp.bfloat16),
        compiler_params=LIMIT,
        name="logits_slices",
    )(both, head)


def back_body(expo_ref, head_ref, out_ref, hv_ref, sem):
    depth, classes = head_ref.shape
    n, _, share = expo_ref.shape
    pieces = sem.shape[0]
    size = classes // pieces
    copies = [
        pltpu.make_async_copy(head_ref.at[:, pl.ds(p * size, size)], hv_ref.at[p], sem.at[p]) for p in range(pieces)
    ]
    for c in copies:
        c.start()
    e = jnp.concatenate([expo_ref[s] for s in range(n)], axis=1)
    total = jnp.sum(e.astype(jnp.float32), axis=1, keepdims=True)
    out_ref[:, depth:] = jnp.broadcast_to(total, (out_ref.shape[0], 128))
    acc = jnp.zeros((out_ref.shape[0], depth), jnp.float32)
    for p in range(pieces):
        copies[p].wait()
        acc += lax.dot_general(
            e[:, p * size : (p + 1) * size], hv_ref[p], NT, preferred_element_type=jnp.float32
        )
    out_ref[:, :depth] = acc


def back(expo, head):
    rows = expo.shape[1]
    depth, classes = head.shape
    pieces = 4
    return pl.pallas_call(
        back_body,
        in_specs=[VM, HB],
        out_specs=VM,
        out_shape=jax.ShapeDtypeStruct((rows, depth + 128), jnp.float32),
        scratch_shapes=[
            pltpu.VMEM((pieces, depth, classes // pieces), head.dtype),
            pltpu.SemaphoreType.DMA((pieces,)),
        ],
        compiler_params=LIMIT,
        name="back",
    )(expo, pltpu.with_memory_space_constraint(head, pltpu.HBM))


def final_body(pos, place_ref, m_ref, part_ref, hot_ref, own_ref, other_ref, out_ref):
    width = hot_ref.shape[3]
    imgs, ka, _ = m_ref.shape
    acc = jnp.zeros(out_ref.shape, jnp.float32)
    for k, pe_ref in enumerate((own_ref, other_ref)):
        h = place_ref[1] if k == 0 else 1 - place_ref[1]
        part = sum(part_ref[a, h] for a in range(part_ref.shape[0]))
        hot = sum(hot_ref[a, h].astype(jnp.float32)[imgs:] for a in range(hot_ref.shape[0]))
        d = part[:, :width] / part[:, width : width + 1] - hot
        d = (d / pos).astype(jnp.bfloat16).astype(jnp.float32)
        lane = pl.multiple_of(h * width, width)
        v = (m_ref[:, :, pl.ds(lane, width)] * d[:, None, :]).reshape(imgs * ka, width)
        v_hi = v.astype(jnp.bfloat16)
        v_lo = (v - v_hi.astype(jnp.float32)).astype(jnp.bfloat16)
        acc += lax.dot_general(v_hi, pe_ref[...], NT, preferred_element_type=jnp.float32)
        acc += lax.dot_general(v_lo, pe_ref[...], NT, preferred_element_type=jnp.float32)
    out_ref[...] = acc


def final(place, m, part, hot, pe_own, pe_other, pos):
    imgs, ka, _ = m.shape
    return pl.pallas_call(
        functools.partial(final_body, pos),
        in_specs=[pl.BlockSpec(memory_space=pltpu.SMEM)] + [VM] * 5,
        out_specs=VM,
        out_shape=jax.ShapeDtypeStruct((imgs * ka, pe_own.shape[0]), jnp.float32),
        compiler_params=LIMIT,
        name="final",
    )(place, m, part, hot, pe_own, pe_other)


def per_device(stream, mid, conv_weight, head_weight, labels, proj_act, proj_err):
    images, pos, width = stream.shape
    kz = mid.shape[2]
    half = images // 2
    nz = lax.axis_size("z")
    parts = nz * 2
    fs = lax.axis_size("yhi") * lax.axis_size("core")
    block = head_weight.shape[1]
    me_y = lax.axis_index("ylo")
    f = lax.axis_index("yhi") * lax.axis_size("core") + lax.axis_index("core")
    swap = [(0, 1), (1, 0)]

    mid = mid.reshape(2, half, pos, kz)
    stream = stream.reshape(2, half, pos, width)
    mine = lax.dynamic_index_in_dim(mid, me_y, 0, keepdims=False)
    theirs = lax.dynamic_index_in_dim(mid, 1 - me_y, 0, keepdims=False)
    swapped = lax.ppermute(theirs, "ylo", swap)
    pe_own = proj_err.T
    sent = lax.dynamic_index_in_dim(stream, 1 - me_y, 0, keepdims=False).reshape(half * pos, width)
    stream_other = lax.ppermute(jnp.concatenate([sent, pe_own], axis=0), "ylo", swap)
    weights = pass_weight(conv_weight)
    got = rings(mine, swapped, nz)

    classes = f * block + jnp.arange(block, dtype=jnp.int32)
    onehot = (labels[:, None] == classes[None, :]).astype(jnp.bfloat16)
    hot = lax.dot_general(onehot, head_weight, NT, preferred_element_type=jnp.float32)
    hot = hot.astype(jnp.bfloat16).reshape(fs, 2, half, width)

    blocks, weights, stream_other, hot = lax.optimization_barrier(([g[2] for g in got], weights, stream_other, hot))
    got = [g[:2] + (b,) for g, b in zip(got, blocks)]
    place = jnp.stack([lax.axis_index(a) for a in ("z", "ylo", "yhi", "core")]).astype(jnp.int32)
    both, mask, acts = conv(
        place, got, weights,
        stream.reshape(2, half * pos, width), stream_other, proj_act.T, hot, nz,
    )

    both = lax.all_to_all(both.reshape(2 * fs, 2 * half, width), ROWS, 0, 0)
    part = lax.all_to_all(logits_slices(both, head_weight, parts), SPREAD, 0, 0)
    mask, both = lax.optimization_barrier((mask, both))
    m = masked_sums(acts, mask)
    pe_other = stream_other[half * pos :]
    part, m, pe_other = lax.optimization_barrier((part, m, pe_other))

    logits = jnp.sum(part.astype(jnp.float32), axis=0)
    expo = jnp.minimum(jnp.exp(logits), BF16_TOP).astype(jnp.bfloat16)
    expo = lax.all_to_all(jnp.broadcast_to(expo, (parts,) + expo.shape), SPREAD, 0, 0)

    part = back(expo, head_weight).reshape(2 * fs, half, width + 128)
    part = lax.all_to_all(part, ROWS, 0, 0).reshape(fs, 2, half, width + 128)

    grads = final(place, m, part, both.reshape(fs, 2, 2 * half, width), pe_own, pe_other, pos)
    grads = grads.reshape(half, nz, 2, -1).transpose(2, 1, 0, 3).reshape(parts, half, -1)
    grads = lax.all_to_all(grads, SPREAD, 0, 0)
    grads = jnp.sum(grads.reshape(2, nz, half, -1), axis=1)
    return grads.reshape(images, -1)


def solution(mesh):
    fine = Mesh(mesh.devices.reshape(4, 8, 2, 2, 2), ("seed", "z", "ylo", "yhi", "core"))
    rows = ("seed", "yhi", "core")
    in_specs = (
        P(rows, None, CHAN),
        P(rows, None, CHAN),
        P(rows, CHAN),
        P(("seed", "z", "ylo"), ("yhi", "core")),
        P(),
        P(),
        P(CHAN, None),
    )
    return jax.shard_map(
        per_device, mesh=fine, in_specs=in_specs, out_specs=P(rows, CHAN), check_vma=False
    )
```

```python
import functools

import jax
import jax.numpy as jnp
from jax import lax
from jax.experimental import pallas as pl
from jax.experimental.pallas import tpu as pltpu
from jax.sharding import Mesh, PartitionSpec as P

CHAN = ("z", "ylo")
SPREAD = ("ylo", "z")
ROWS = ("yhi", "core", "ylo")
BF16_TOP = 3.3895313892515355e38
NT = (((1,), (1,)), ((), ()))
TN = (((0,), (0,)), ((), ()))
VM = pl.BlockSpec(memory_space=pltpu.VMEM)
HB = pl.BlockSpec(memory_space=pltpu.HBM)
LIMIT = pltpu.CompilerParams(vmem_limit_bytes=16 * 1024 * 1024)


def rings(mine, swapped, nz, w, early):
    right = [(i, (i + 1) % nz) for i in range(nz)]
    left = [(i, (i - 1) % nz) for i in range(nz)]
    r = lax.ppermute(mine, "z", right)
    l = lax.ppermute(mine, "z", left)
    r, l, swapped, w = lax.optimization_barrier((r, l, swapped, w))
    swap = [(0, 1), (1, 0)]
    across = [(i, 3 - i) for i in range(4)]
    low = lax.ppermute(w, "ylo", swap)
    high = lax.ppermute(w, ("ylo", "yhi"), across)
    arrays = [mine, swapped, r, l]
    plan = [(0, None, 0, 0), (1, None, 1, 0), (2, None, 0, 1), (3, None, 0, nz - 1)]
    r = jnp.stack([r, swapped])
    l = jnp.stack([l, swapped])
    for k in range(2, nz // 2):
        r = lax.ppermute(r, "z", right)
        l = lax.ppermute(l, "z", left)
        if k == 2:
            far = lax.ppermute(lax.optimization_barrier((low, r, l))[0], ("ylo", "yhi"), across)
        if k == nz // 2 - 1:
            every = jnp.stack(lax.optimization_barrier((w, far, low, high, r, l, early))[:4])
            weights = [every, lax.ppermute(every, "core", swap)]
        for way, v in ((1, r), (-1, l)):
            plan += [(len(arrays), 0, 0, way * k % nz), (len(arrays), 1, 1, way * (k - 1) % nz)]
            arrays.append(v)
    last = nz // 2
    r = lax.ppermute(r, "z", right)
    plan += [(len(arrays), 0, 0, last), (len(arrays), 1, 1, last - 1)]
    arrays.append(r)
    l = l[1]
    for k in (last + 1, last):
        l = lax.ppermute(l, "z", left)
        plan.append((len(arrays), None, 1, k))
        arrays.append(l)
    return arrays, weights, tuple(plan)


def conv_body(nz, count, plan, place_ref, *refs):
    blocks = refs[:count]
    w_refs = refs[count : count + 2]
    own_ref, first_ref, rest_ref, pa_ref, hot_ref, pooled_ref, mask_ref, acts_ref = refs[count + 2 : count + 10]
    x_ref, wv_ref, sv_ref, mv_ref, x_sem, w_sem, s_sem, m_sem = refs[count + 10 :]
    imgs, pos, kz = blocks[0].shape
    cut = imgs // 2
    ka = pa_ref.shape[0]
    depth, width = wv_ref.shape[1:]
    rows_w = w_refs[0].shape[1]
    me_z = place_ref[0]
    me_y = place_ref[1]
    me_hi = place_ref[2]
    me_core = place_ref[3]
    columns = (me_y, 1 - me_y)

    def copy_x(part):
        span = pl.ds(part * cut, cut)
        made = []
        for i, (array, place, sub, shift) in enumerate(plan):
            ref = blocks[array] if place is None else blocks[array].at[place]
            source = lax.rem(me_z + (nz - shift), nz)
            lane = pl.multiple_of((source * 2 + columns[sub]) * kz, kz)
            made.append(
                pltpu.make_async_copy(ref.at[span], x_ref.at[span, :, pl.ds(lane, kz)], x_sem.at[part, i])
            )
        return made

    def copy_w(h):
        made = []
        for i in range(2):
            hi = me_hi if i == 0 else 1 - me_hi
            for k in range(2):
                core = me_core if k == 0 else 1 - me_core
                row = pl.multiple_of((hi * 2 + core) * rows_w, rows_w)
                made.append(
                    pltpu.make_async_copy(
                        w_refs[k].at[2 * h + i], wv_ref.at[h, pl.ds(row, rows_w)], w_sem.at[h, 2 * i + k]
                    )
                )
        return made

    copies = [copy_w(0) + copy_x(0), copy_x(1), copy_w(1)]
    edge = first_ref.shape[0]
    streams = [
        [pltpu.make_async_copy(own_ref.at[me_y], sv_ref.at[0], s_sem.at[0])],
        [
            pltpu.make_async_copy(first_ref, sv_ref.at[1, pl.ds(0, edge)], s_sem.at[1]),
            pltpu.make_async_copy(
                rest_ref.at[pl.ds(0, imgs * pos - edge)], sv_ref.at[1, pl.ds(edge, imgs * pos - edge)], s_sem.at[2]
            ),
        ],
    ]
    for c in copies[0] + streams[0] + copies[1] + copies[2] + streams[1]:
        c.start()
    pooled_ref[:, :, imgs:] = hot_ref[...]
    sends = []
    for h in range(2):
        for part in range(2):
            if h == 0:
                for c in copies[part]:
                    c.wait()
            elif part == 0:
                for c in copies[2]:
                    c.wait()
            x = x_ref[part * cut : (part + 1) * cut].reshape(cut * pos, depth)
            y = jnp.dot(x, wv_ref[h], preferred_element_type=jnp.float32)
            if h == 0:
                acts = lax.dot_general(x, pa_ref[...], NT, preferred_element_type=jnp.float32)
                hi = acts.astype(jnp.bfloat16)
                here = slice(part * cut * pos, (part + 1) * cut * pos)
                acts_ref[here, :ka] = hi
                acts_ref[here, ka:] = (acts - hi.astype(jnp.float32)).astype(jnp.bfloat16)
            if part == 0:
                for c in streams[h]:
                    c.wait()
            y = (y + sv_ref[h, part * cut * pos : (part + 1) * cut * pos].astype(jnp.float32)).reshape(cut, pos, width)
            pooled = (jnp.sum(jnp.maximum(y, 0.0), axis=1) / pos).astype(jnp.bfloat16)
            for f in range(pooled_ref.shape[0]):
                pooled_ref[f, columns[h], part * cut : (part + 1) * cut] = pooled
            mv_ref[h, part] = jnp.where(y > 0.0, 1.0, 0.0).astype(jnp.bfloat16)
            sends.append(
                pltpu.make_async_copy(
                    mv_ref.at[h, part], mask_ref.at[columns[h], pl.ds(part * cut, cut)], m_sem.at[h, part]
                )
            )
            sends[-1].start()
    for c in sends:
        c.wait()


def conv(place, blocks, plan, weights, stream2, stream_first, stream_rest, proj_act, hot, nz):
    half, pos, kz = blocks[0].shape
    fs, _, _, width = hot.shape
    ka, depth = proj_act.shape
    return pl.pallas_call(
        functools.partial(conv_body, nz, len(blocks), plan),
        in_specs=[pl.BlockSpec(memory_space=pltpu.SMEM)] + [HB] * (len(blocks) + 5) + [VM, VM],
        out_specs=[VM, HB, VM],
        out_shape=[
            jax.ShapeDtypeStruct((fs, 2, 2 * half, width), jnp.bfloat16),
            jax.ShapeDtypeStruct((2, half, pos, width), jnp.bfloat16),
            jax.ShapeDtypeStruct((half * pos, 2 * ka), jnp.bfloat16),
        ],
        scratch_shapes=[
            pltpu.VMEM((half, pos, depth), jnp.bfloat16),
            pltpu.VMEM((2, depth, width), jnp.bfloat16),
            pltpu.VMEM((2, half * pos, width), jnp.bfloat16),
            pltpu.VMEM((2, 2, half // 2, pos, width), jnp.bfloat16),
            pltpu.SemaphoreType.DMA((2, len(plan))),
            pltpu.SemaphoreType.DMA((2, 4)),
            pltpu.SemaphoreType.DMA((3,)),
            pltpu.SemaphoreType.DMA((2, 2)),
        ],
        compiler_params=pltpu.CompilerParams(vmem_limit_bytes=32 * 1024 * 1024),
        name="conv_pool_mask",
    )(place, *[pltpu.with_memory_space_constraint(b, pltpu.HBM) for b in (*blocks, *weights, stream2, stream_first, stream_rest)], proj_act, hot)


def masked_body(acts_ref, mask_ref, m_ref):
    _, imgs, pos, _ = mask_ref.shape
    ka = m_ref.shape[1]
    for i in range(imgs):
        both = lax.dot_general(
            acts_ref[i * pos : (i + 1) * pos, :], mask_ref[0, i], TN, preferred_element_type=jnp.float32
        )
        m_ref[i] = both[:ka] + both[ka:]


def masked_sums(acts, mask):
    two, imgs, pos, width = mask.shape
    ka = acts.shape[1] // 2
    return pl.pallas_call(
        masked_body,
        grid=(two,),
        in_specs=[
            pl.BlockSpec(acts.shape, lambda h: (0, 0)),
            pl.BlockSpec((1, imgs, pos, width), lambda h: (h, 0, 0, 0)),
        ],
        out_specs=pl.BlockSpec((imgs, ka, width), lambda h: (0, 0, h)),
        out_shape=jax.ShapeDtypeStruct((imgs, ka, two * width), jnp.float32),
        compiler_params=LIMIT,
        name="masked_sums",
    )(acts, mask)


def logits_body(both_ref, head_ref, out_ref):
    share = out_ref.shape[2]
    some, rows, width = both_ref.shape
    pooled = both_ref[:, : rows // 2].astype(jnp.float32).reshape(some * rows // 2, width).astype(jnp.bfloat16)
    for s in range(out_ref.shape[0]):
        part = jnp.dot(pooled, head_ref[:, s * share : (s + 1) * share], preferred_element_type=jnp.float32)
        out_ref[s] = part.astype(jnp.bfloat16)


def logits_slices(both, head, n):
    some, rows, _ = both.shape
    return pl.pallas_call(
        logits_body,
        in_specs=[VM, VM],
        out_specs=VM,
        out_shape=jax.ShapeDtypeStruct((n, some * rows // 2, head.shape[1] // n), jnp.bfloat16),
        compiler_params=LIMIT,
        name="logits_slices",
    )(both, head)


def back_body(expo_ref, head_ref, out_ref, hv_ref, sem):
    depth, classes = head_ref.shape
    n, _, share = expo_ref.shape
    pieces = sem.shape[0]
    size = classes // pieces
    copies = [
        pltpu.make_async_copy(head_ref.at[:, pl.ds(p * size, size)], hv_ref.at[p], sem.at[p]) for p in range(pieces)
    ]
    for c in copies:
        c.start()
    e = jnp.concatenate([expo_ref[s] for s in range(n)], axis=1)
    total = jnp.sum(e.astype(jnp.float32), axis=1, keepdims=True)
    out_ref[:, depth:] = jnp.broadcast_to(total, (out_ref.shape[0], 128))
    acc = jnp.zeros((out_ref.shape[0], depth), jnp.float32)
    for p in range(pieces):
        copies[p].wait()
        acc += lax.dot_general(
            e[:, p * size : (p + 1) * size], hv_ref[p], NT, preferred_element_type=jnp.float32
        )
    out_ref[:, :depth] = acc


def back(expo, head):
    rows = expo.shape[1]
    depth, classes = head.shape
    pieces = 4
    return pl.pallas_call(
        back_body,
        in_specs=[VM, HB],
        out_specs=VM,
        out_shape=jax.ShapeDtypeStruct((rows, depth + 128), jnp.float32),
        scratch_shapes=[
            pltpu.VMEM((pieces, depth, classes // pieces), head.dtype),
            pltpu.SemaphoreType.DMA((pieces,)),
        ],
        compiler_params=LIMIT,
        name="back",
    )(expo, pltpu.with_memory_space_constraint(head, pltpu.HBM))


def final_body(pos, place_ref, m_ref, part_ref, hot_ref, own_ref, other_ref, out_ref):
    width = hot_ref.shape[3]
    imgs, ka, _ = m_ref.shape
    acc = jnp.zeros(out_ref.shape, jnp.float32)
    for k, pe_ref in enumerate((own_ref, other_ref)):
        h = place_ref[1] if k == 0 else 1 - place_ref[1]
        part = sum(part_ref[a, h] for a in range(part_ref.shape[0]))
        hot = sum(hot_ref[a, h].astype(jnp.float32)[imgs:] for a in range(hot_ref.shape[0]))
        d = part[:, :width] / part[:, width : width + 1] - hot
        d = (d / pos).astype(jnp.bfloat16).astype(jnp.float32)
        lane = pl.multiple_of(h * width, width)
        v = (m_ref[:, :, pl.ds(lane, width)] * d[:, None, :]).reshape(imgs * ka, width)
        v_hi = v.astype(jnp.bfloat16)
        v_lo = (v - v_hi.astype(jnp.float32)).astype(jnp.bfloat16)
        acc += lax.dot_general(v_hi, pe_ref[...], NT, preferred_element_type=jnp.float32)
        acc += lax.dot_general(v_lo, pe_ref[...], NT, preferred_element_type=jnp.float32)
    out_ref[...] = acc


def final(place, m, part, hot, pe_own, pe_other, pos):
    imgs, ka, _ = m.shape
    return pl.pallas_call(
        functools.partial(final_body, pos),
        in_specs=[pl.BlockSpec(memory_space=pltpu.SMEM)] + [VM] * 5,
        out_specs=VM,
        out_shape=jax.ShapeDtypeStruct((imgs * ka, pe_own.shape[0]), jnp.float32),
        compiler_params=LIMIT,
        name="final",
    )(place, m, part, hot, pe_own, pe_other)


def per_device(stream, mid, conv_weight, head_weight, labels, proj_act, proj_err):
    images, pos, width = stream.shape
    kz = mid.shape[2]
    half = images // 2
    nz = lax.axis_size("z")
    parts = nz * 2
    fs = lax.axis_size("yhi") * lax.axis_size("core")
    block = head_weight.shape[1]
    me_y = lax.axis_index("ylo")
    f = lax.axis_index("yhi") * lax.axis_size("core") + lax.axis_index("core")
    swap = [(0, 1), (1, 0)]

    mid = mid.reshape(2, half, pos, kz)
    stream = stream.reshape(2, half, pos, width)
    mine = lax.dynamic_index_in_dim(mid, me_y, 0, keepdims=False)
    theirs = lax.dynamic_index_in_dim(mid, 1 - me_y, 0, keepdims=False)
    swapped = lax.ppermute(theirs, "ylo", swap)
    pe_own = proj_err.T
    sent = lax.dynamic_index_in_dim(stream, 1 - me_y, 0, keepdims=False).reshape(half * pos, width)
    cut = (half * pos + pe_own.shape[0]) // 2
    stream_first = lax.ppermute(sent[:cut], "ylo", swap)
    stream_rest = lax.ppermute(jnp.concatenate([sent[cut:], pe_own], axis=0), "ylo", swap)
    blocks, weights, plan = rings(mine, swapped, nz, conv_weight, stream_first)

    classes = f * block + jnp.arange(block, dtype=jnp.int32)
    onehot = (labels[:, None] == classes[None, :]).astype(jnp.bfloat16)
    hot = lax.dot_general(onehot, head_weight, NT, preferred_element_type=jnp.float32)
    hot = hot.astype(jnp.bfloat16).reshape(fs, 2, half, width)

    blocks, weights, stream_rest, hot = lax.optimization_barrier((blocks, weights, stream_rest, hot))
    place = jnp.stack([lax.axis_index(a) for a in ("z", "ylo", "yhi", "core")]).astype(jnp.int32)
    both, mask, acts = conv(
        place, blocks, plan, weights,
        stream.reshape(2, half * pos, width), stream_first, stream_rest, proj_act.T, hot, nz,
    )

    both = lax.all_to_all(both.reshape(2 * fs, 2 * half, width), ROWS, 0, 0)
    part = lax.all_to_all(logits_slices(both, head_weight, parts), SPREAD, 0, 0)
    mask, both = lax.optimization_barrier((mask, both))
    m = masked_sums(acts, mask)
    pe_other = stream_rest[half * pos - cut :]
    part, m, pe_other = lax.optimization_barrier((part, m, pe_other))

    logits = jnp.sum(part.astype(jnp.float32), axis=0)
    expo = jnp.minimum(jnp.exp(logits), BF16_TOP).astype(jnp.bfloat16)
    expo = lax.all_to_all(jnp.broadcast_to(expo, (parts,) + expo.shape), SPREAD, 0, 0)

    part = back(expo, head_weight).reshape(2 * fs, half, width + 128)
    part = lax.all_to_all(part, ROWS, 0, 0).reshape(fs, 2, half, width + 128)

    grads = final(place, m, part, both.reshape(fs, 2, 2 * half, width), pe_own, pe_other, pos)
    grads = grads.reshape(half, nz, 2, -1).transpose(2, 1, 0, 3).reshape(parts, half, -1)
    grads = lax.all_to_all(grads, SPREAD, 0, 0)
    grads = jnp.sum(grads.reshape(2, nz, half, -1), axis=1)
    return grads.reshape(images, -1)


def solution(mesh):
    fine = Mesh(mesh.devices.reshape(4, 8, 2, 2, 2), ("seed", "z", "ylo", "yhi", "core"))
    rows = ("seed", "yhi", "core")
    in_specs = (
        P(rows, None, CHAN),
        P(rows, None, CHAN),
        P(rows, CHAN),
        P(("seed", "z", "ylo"), ("yhi", "core")),
        P(),
        P(),
        P(CHAN, None),
    )
    return jax.shard_map(
        per_device, mesh=fine, in_specs=in_specs, out_specs=P(rows, CHAN), check_vma=False
    )
```

```python
import functools

import jax
import jax.numpy as jnp
from jax import lax
from jax.experimental import pallas as pl
from jax.experimental.pallas import tpu as pltpu
from jax.sharding import Mesh, PartitionSpec as P

CHAN = ("z", "ylo")
SPREAD = ("ylo", "z")
ROWS = ("yhi", "core", "ylo")
BF16_TOP = 3.3895313892515355e38
NT = (((1,), (1,)), ((), ()))
TN = (((0,), (0,)), ((), ()))
VM = pl.BlockSpec(memory_space=pltpu.VMEM)
HB = pl.BlockSpec(memory_space=pltpu.HBM)
LIMIT = pltpu.CompilerParams(vmem_limit_bytes=16 * 1024 * 1024)


def rings(mine, swapped, nz, w, early):
    right = [(i, (i + 1) % nz) for i in range(nz)]
    left = [(i, (i - 1) % nz) for i in range(nz)]
    r = lax.ppermute(mine, "z", right)
    l = lax.ppermute(mine, "z", left)
    r, l, swapped, w = lax.optimization_barrier((r, l, swapped, w))
    swap = [(0, 1), (1, 0)]
    across = [(i, 3 - i) for i in range(4)]
    low = lax.ppermute(w, "ylo", swap)
    high = lax.ppermute(w, ("ylo", "yhi"), across)
    arrays = [mine, swapped, r, l]
    plan = [(0, None, 0, 0), (1, None, 1, 0), (2, None, 0, 1), (3, None, 0, nz - 1)]
    r = jnp.stack([r, swapped])
    l = jnp.stack([l, swapped])
    for k in range(2, nz // 2):
        r = lax.ppermute(r, "z", right)
        l = lax.ppermute(l, "z", left)
        if k == 2:
            r, l, low, high = lax.optimization_barrier((r, l, low, high))
            far = lax.ppermute(low, ("ylo", "yhi"), across)
        elif k == nz // 2 - 1:
            r, l, far, early = lax.optimization_barrier((r, l, far, early))
            every = jnp.stack([w, far, low, high])
            weights = [every, lax.ppermute(every, "core", swap)]
        for way, v in ((1, r), (-1, l)):
            plan += [(len(arrays), 0, 0, way * k % nz), (len(arrays), 1, 1, way * (k - 1) % nz)]
            arrays.append(v)
    last = nz // 2
    r = lax.ppermute(r, "z", right)
    plan += [(len(arrays), 0, 0, last), (len(arrays), 1, 1, last - 1)]
    arrays.append(r)
    l = l[1]
    for k in (last + 1, last):
        l = lax.ppermute(l, "z", left)
        plan.append((len(arrays), None, 1, k))
        arrays.append(l)
    return arrays, weights, tuple(plan)


def conv_body(nz, count, plan, place_ref, *refs):
    blocks = refs[:count]
    w_refs = refs[count : count + 2]
    own_ref, first_ref, rest_ref, pa_ref, hot_ref, pooled_ref, mask_ref, acts_ref = refs[count + 2 : count + 10]
    x_ref, wv_ref, sv_ref, mv_ref, x_sem, w_sem, s_sem, m_sem = refs[count + 10 :]
    imgs, pos, kz = blocks[0].shape
    cut = imgs // 2
    ka = pa_ref.shape[0]
    depth, width = wv_ref.shape[1:]
    rows_w = w_refs[0].shape[1]
    me_z = place_ref[0]
    me_y = place_ref[1]
    me_hi = place_ref[2]
    me_core = place_ref[3]
    columns = (me_y, 1 - me_y)

    def copy_x(part):
        span = pl.ds(part * cut, cut)
        made = []
        for i, (array, place, sub, shift) in enumerate(plan):
            ref = blocks[array] if place is None else blocks[array].at[place]
            source = lax.rem(me_z + (nz - shift), nz)
            lane = pl.multiple_of((source * 2 + columns[sub]) * kz, kz)
            made.append(
                pltpu.make_async_copy(ref.at[span], x_ref.at[span, :, pl.ds(lane, kz)], x_sem.at[part, i])
            )
        return made

    def copy_w(h):
        made = []
        for i in range(2):
            hi = me_hi if i == 0 else 1 - me_hi
            for k in range(2):
                core = me_core if k == 0 else 1 - me_core
                row = pl.multiple_of((hi * 2 + core) * rows_w, rows_w)
                made.append(
                    pltpu.make_async_copy(
                        w_refs[k].at[2 * h + i], wv_ref.at[h, pl.ds(row, rows_w)], w_sem.at[h, 2 * i + k]
                    )
                )
        return made

    copies = [copy_w(0) + copy_x(0), copy_x(1), copy_w(1)]
    edge = first_ref.shape[0]
    streams = [
        [pltpu.make_async_copy(own_ref.at[me_y], sv_ref.at[0], s_sem.at[0])],
        [
            pltpu.make_async_copy(first_ref, sv_ref.at[1, pl.ds(0, edge)], s_sem.at[1]),
            pltpu.make_async_copy(
                rest_ref.at[pl.ds(0, imgs * pos - edge)], sv_ref.at[1, pl.ds(edge, imgs * pos - edge)], s_sem.at[2]
            ),
        ],
    ]
    for c in copies[0] + streams[0] + copies[1] + copies[2] + streams[1]:
        c.start()
    pooled_ref[:, :, imgs:] = hot_ref[...]
    sends = []
    for h in range(2):
        for part in range(2):
            if h == 0:
                for c in copies[part]:
                    c.wait()
            elif part == 0:
                for c in copies[2]:
                    c.wait()
            x = x_ref[part * cut : (part + 1) * cut].reshape(cut * pos, depth)
            y = jnp.dot(x, wv_ref[h], preferred_element_type=jnp.float32)
            if h == 0:
                acts = lax.dot_general(x, pa_ref[...], NT, preferred_element_type=jnp.float32)
                hi = acts.astype(jnp.bfloat16)
                here = slice(part * cut * pos, (part + 1) * cut * pos)
                acts_ref[here, :ka] = hi
                acts_ref[here, ka:] = (acts - hi.astype(jnp.float32)).astype(jnp.bfloat16)
            if part == 0:
                for c in streams[h]:
                    c.wait()
            y = (y + sv_ref[h, part * cut * pos : (part + 1) * cut * pos].astype(jnp.float32)).reshape(cut, pos, width)
            pooled = (jnp.sum(jnp.maximum(y, 0.0), axis=1) / pos).astype(jnp.bfloat16)
            for f in range(pooled_ref.shape[0]):
                pooled_ref[f, columns[h], part * cut : (part + 1) * cut] = pooled
            mv_ref[h, part] = jnp.where(y > 0.0, 1.0, 0.0).astype(jnp.bfloat16)
            sends.append(
                pltpu.make_async_copy(
                    mv_ref.at[h, part], mask_ref.at[columns[h], pl.ds(part * cut, cut)], m_sem.at[h, part]
                )
            )
            sends[-1].start()
    for c in sends:
        c.wait()


def conv(place, blocks, plan, weights, stream2, stream_first, stream_rest, proj_act, hot, nz):
    half, pos, kz = blocks[0].shape
    fs, _, _, width = hot.shape
    ka, depth = proj_act.shape
    return pl.pallas_call(
        functools.partial(conv_body, nz, len(blocks), plan),
        in_specs=[pl.BlockSpec(memory_space=pltpu.SMEM)] + [HB] * (len(blocks) + 5) + [VM, VM],
        out_specs=[VM, HB, VM],
        out_shape=[
            jax.ShapeDtypeStruct((fs, 2, 2 * half, width), jnp.bfloat16),
            jax.ShapeDtypeStruct((2, half, pos, width), jnp.bfloat16),
            jax.ShapeDtypeStruct((half * pos, 2 * ka), jnp.bfloat16),
        ],
        scratch_shapes=[
            pltpu.VMEM((half, pos, depth), jnp.bfloat16),
            pltpu.VMEM((2, depth, width), jnp.bfloat16),
            pltpu.VMEM((2, half * pos, width), jnp.bfloat16),
            pltpu.VMEM((2, 2, half // 2, pos, width), jnp.bfloat16),
            pltpu.SemaphoreType.DMA((2, len(plan))),
            pltpu.SemaphoreType.DMA((2, 4)),
            pltpu.SemaphoreType.DMA((3,)),
            pltpu.SemaphoreType.DMA((2, 2)),
        ],
        compiler_params=pltpu.CompilerParams(vmem_limit_bytes=32 * 1024 * 1024),
        name="conv_pool_mask",
    )(place, *[pltpu.with_memory_space_constraint(b, pltpu.HBM) for b in (*blocks, *weights, stream2, stream_first, stream_rest)], proj_act, hot)


def masked_body(acts_ref, mask_ref, m_ref):
    _, imgs, pos, _ = mask_ref.shape
    ka = m_ref.shape[1]
    for i in range(imgs):
        both = lax.dot_general(
            acts_ref[i * pos : (i + 1) * pos, :], mask_ref[0, i], TN, preferred_element_type=jnp.float32
        )
        m_ref[i] = both[:ka] + both[ka:]


def masked_sums(acts, mask):
    two, imgs, pos, width = mask.shape
    ka = acts.shape[1] // 2
    return pl.pallas_call(
        masked_body,
        grid=(two,),
        in_specs=[
            pl.BlockSpec(acts.shape, lambda h: (0, 0)),
            pl.BlockSpec((1, imgs, pos, width), lambda h: (h, 0, 0, 0)),
        ],
        out_specs=pl.BlockSpec((imgs, ka, width), lambda h: (0, 0, h)),
        out_shape=jax.ShapeDtypeStruct((imgs, ka, two * width), jnp.float32),
        compiler_params=LIMIT,
        name="masked_sums",
    )(acts, mask)


def logits_body(both_ref, head_ref, out_ref):
    share = out_ref.shape[2]
    some, rows, width = both_ref.shape
    pooled = both_ref[:, : rows // 2].astype(jnp.float32).reshape(some * rows // 2, width).astype(jnp.bfloat16)
    for s in range(out_ref.shape[0]):
        part = jnp.dot(pooled, head_ref[:, s * share : (s + 1) * share], preferred_element_type=jnp.float32)
        out_ref[s] = part.astype(jnp.bfloat16)


def logits_slices(both, head, n):
    some, rows, _ = both.shape
    return pl.pallas_call(
        logits_body,
        in_specs=[VM, VM],
        out_specs=VM,
        out_shape=jax.ShapeDtypeStruct((n, some * rows // 2, head.shape[1] // n), jnp.bfloat16),
        compiler_params=LIMIT,
        name="logits_slices",
    )(both, head)


def back_body(expo_ref, head_ref, out_ref, hv_ref, sem):
    depth, classes = head_ref.shape
    n, _, share = expo_ref.shape
    pieces = sem.shape[0]
    size = classes // pieces
    copies = [
        pltpu.make_async_copy(head_ref.at[:, pl.ds(p * size, size)], hv_ref.at[p], sem.at[p]) for p in range(pieces)
    ]
    for c in copies:
        c.start()
    e = jnp.concatenate([expo_ref[s] for s in range(n)], axis=1)
    total = jnp.sum(e.astype(jnp.float32), axis=1, keepdims=True)
    out_ref[:, depth:] = jnp.broadcast_to(total, (out_ref.shape[0], 128))
    acc = jnp.zeros((out_ref.shape[0], depth), jnp.float32)
    for p in range(pieces):
        copies[p].wait()
        acc += lax.dot_general(
            e[:, p * size : (p + 1) * size], hv_ref[p], NT, preferred_element_type=jnp.float32
        )
    out_ref[:, :depth] = acc


def back(expo, head):
    rows = expo.shape[1]
    depth, classes = head.shape
    pieces = 4
    return pl.pallas_call(
        back_body,
        in_specs=[VM, HB],
        out_specs=VM,
        out_shape=jax.ShapeDtypeStruct((rows, depth + 128), jnp.float32),
        scratch_shapes=[
            pltpu.VMEM((pieces, depth, classes // pieces), head.dtype),
            pltpu.SemaphoreType.DMA((pieces,)),
        ],
        compiler_params=LIMIT,
        name="back",
    )(expo, pltpu.with_memory_space_constraint(head, pltpu.HBM))


def final_body(pos, place_ref, m_ref, part_ref, hot_ref, own_ref, other_ref, out_ref):
    width = hot_ref.shape[3]
    imgs, ka, _ = m_ref.shape
    acc = jnp.zeros(out_ref.shape, jnp.float32)
    for k, pe_ref in enumerate((own_ref, other_ref)):
        h = place_ref[1] if k == 0 else 1 - place_ref[1]
        part = sum(part_ref[a, h] for a in range(part_ref.shape[0]))
        hot = sum(hot_ref[a, h].astype(jnp.float32)[imgs:] for a in range(hot_ref.shape[0]))
        d = part[:, :width] / part[:, width : width + 1] - hot
        d = (d / pos).astype(jnp.bfloat16).astype(jnp.float32)
        lane = pl.multiple_of(h * width, width)
        v = (m_ref[:, :, pl.ds(lane, width)] * d[:, None, :]).reshape(imgs * ka, width)
        v_hi = v.astype(jnp.bfloat16)
        v_lo = (v - v_hi.astype(jnp.float32)).astype(jnp.bfloat16)
        acc += lax.dot_general(v_hi, pe_ref[...], NT, preferred_element_type=jnp.float32)
        acc += lax.dot_general(v_lo, pe_ref[...], NT, preferred_element_type=jnp.float32)
    out_ref[...] = acc


def final(place, m, part, hot, pe_own, pe_other, pos):
    imgs, ka, _ = m.shape
    return pl.pallas_call(
        functools.partial(final_body, pos),
        in_specs=[pl.BlockSpec(memory_space=pltpu.SMEM)] + [VM] * 5,
        out_specs=VM,
        out_shape=jax.ShapeDtypeStruct((imgs * ka, pe_own.shape[0]), jnp.float32),
        compiler_params=LIMIT,
        name="final",
    )(place, m, part, hot, pe_own, pe_other)


def per_device(stream, mid, conv_weight, head_weight, labels, proj_act, proj_err):
    images, pos, width = stream.shape
    kz = mid.shape[2]
    half = images // 2
    nz = lax.axis_size("z")
    parts = nz * 2
    fs = lax.axis_size("yhi") * lax.axis_size("core")
    block = head_weight.shape[1]
    me_y = lax.axis_index("ylo")
    f = lax.axis_index("yhi") * lax.axis_size("core") + lax.axis_index("core")
    swap = [(0, 1), (1, 0)]

    mid = mid.reshape(2, half, pos, kz)
    stream = stream.reshape(2, half, pos, width)
    mine = lax.dynamic_index_in_dim(mid, me_y, 0, keepdims=False)
    theirs = lax.dynamic_index_in_dim(mid, 1 - me_y, 0, keepdims=False)
    swapped = lax.ppermute(theirs, "ylo", swap)
    pe_own = proj_err.T
    sent = lax.dynamic_index_in_dim(stream, 1 - me_y, 0, keepdims=False).reshape(half * pos, width)
    cut = (half * pos + pe_own.shape[0]) // 2
    stream_first = lax.ppermute(sent[:cut], "ylo", swap)
    stream_rest = lax.ppermute(jnp.concatenate([sent[cut:], pe_own], axis=0), "ylo", swap)
    blocks, weights, plan = rings(mine, swapped, nz, conv_weight, stream_first)

    classes = f * block + jnp.arange(block, dtype=jnp.int32)
    onehot = (labels[:, None] == classes[None, :]).astype(jnp.bfloat16)
    hot = lax.dot_general(onehot, head_weight, NT, preferred_element_type=jnp.float32)
    hot = hot.astype(jnp.bfloat16).reshape(fs, 2, half, width)

    blocks, weights, stream_rest, hot = lax.optimization_barrier((blocks, weights, stream_rest, hot))
    place = jnp.stack([lax.axis_index(a) for a in ("z", "ylo", "yhi", "core")]).astype(jnp.int32)
    both, mask, acts = conv(
        place, blocks, plan, weights,
        stream.reshape(2, half * pos, width), stream_first, stream_rest, proj_act.T, hot, nz,
    )

    both = lax.all_to_all(both.reshape(2 * fs, 2 * half, width), ROWS, 0, 0)
    part = lax.all_to_all(logits_slices(both, head_weight, parts), SPREAD, 0, 0)
    mask, both = lax.optimization_barrier((mask, both))
    m = masked_sums(acts, mask)
    pe_other = stream_rest[half * pos - cut :]
    part, m, pe_other = lax.optimization_barrier((part, m, pe_other))

    logits = jnp.sum(part.astype(jnp.float32), axis=0)
    expo = jnp.minimum(jnp.exp(logits), BF16_TOP).astype(jnp.bfloat16)
    expo = lax.all_to_all(jnp.broadcast_to(expo, (parts,) + expo.shape), SPREAD, 0, 0)

    part = back(expo, head_weight).reshape(2 * fs, half, width + 128)
    part = lax.all_to_all(part, ROWS, 0, 0).reshape(fs, 2, half, width + 128)

    grads = final(place, m, part, both.reshape(fs, 2, 2 * half, width), pe_own, pe_other, pos)
    grads = grads.reshape(half, nz, 2, -1).transpose(2, 1, 0, 3).reshape(parts, half, -1)
    grads = lax.all_to_all(grads, SPREAD, 0, 0)
    grads = jnp.sum(grads.reshape(2, nz, half, -1), axis=1)
    return grads.reshape(images, -1)


def solution(mesh):
    fine = Mesh(mesh.devices.reshape(4, 8, 2, 2, 2), ("seed", "z", "ylo", "yhi", "core"))
    rows = ("seed", "yhi", "core")
    in_specs = (
        P(rows, None, CHAN),
        P(rows, None, CHAN),
        P(rows, CHAN),
        P(("seed", "z", "ylo"), ("yhi", "core")),
        P(),
        P(),
        P(CHAN, None),
    )
    return jax.shard_map(
        per_device, mesh=fine, in_specs=in_specs, out_specs=P(rows, CHAN), check_vma=False
    )
```

```python
import functools

import jax
import jax.numpy as jnp
from jax import lax
from jax.experimental import pallas as pl
from jax.experimental.pallas import tpu as pltpu
from jax.sharding import Mesh, PartitionSpec as P

CHAN = ("z", "ylo")
SPREAD = ("ylo", "z")
ROWS = ("yhi", "core", "ylo")
BF16_TOP = 3.3895313892515355e38
NT = (((1,), (1,)), ((), ()))
TN = (((0,), (0,)), ((), ()))
VM = pl.BlockSpec(memory_space=pltpu.VMEM)
HB = pl.BlockSpec(memory_space=pltpu.HBM)
LIMIT = pltpu.CompilerParams(vmem_limit_bytes=16 * 1024 * 1024)


def rings(mine, swapped, nz, w, early):
    right = [(i, (i + 1) % nz) for i in range(nz)]
    left = [(i, (i - 1) % nz) for i in range(nz)]
    r = lax.ppermute(mine, "z", right)
    l = lax.ppermute(mine, "z", left)
    r, l, swapped, w = lax.optimization_barrier((r, l, swapped, w))
    swap = [(0, 1), (1, 0)]
    across = [(i, 3 - i) for i in range(4)]
    low = lax.ppermute(w, "ylo", swap)
    high = lax.ppermute(w, ("ylo", "yhi"), across)
    arrays = [mine, swapped, r, l]
    plan = [(0, None, 0, 0), (1, None, 1, 0), (2, None, 0, 1), (3, None, 0, nz - 1)]
    r = jnp.stack([r, swapped])
    l = jnp.stack([l, swapped])
    for k in range(2, nz // 2):
        r = lax.ppermute(r, "z", right)
        l = lax.ppermute(l, "z", left)
        if k == 2:
            r, l = lax.optimization_barrier((r, l))
            low, high, *_ = lax.optimization_barrier((low, high, r, l))
            far = lax.ppermute(low, ("ylo", "yhi"), across)
        elif k == nz // 2 - 1:
            r, l, far, early = lax.optimization_barrier((r, l, far, early))
            every = jnp.stack([w, far, low, high])
            weights = [every, lax.ppermute(every, "core", swap)]
        for way, v in ((1, r), (-1, l)):
            plan += [(len(arrays), 0, 0, way * k % nz), (len(arrays), 1, 1, way * (k - 1) % nz)]
            arrays.append(v)
    last = nz // 2
    r = lax.ppermute(r, "z", right)
    plan += [(len(arrays), 0, 0, last), (len(arrays), 1, 1, last - 1)]
    arrays.append(r)
    l = l[1]
    for k in (last + 1, last):
        l = lax.ppermute(l, "z", left)
        plan.append((len(arrays), None, 1, k))
        arrays.append(l)
    return arrays, weights, tuple(plan)


def block_copies(nz, blocks, plan, place_ref, x_ref, sem, span):
    kz = blocks[0].shape[2]
    made = []
    for i, (array, at, sub, shift) in enumerate(plan):
        ref = blocks[array] if at is None else blocks[array].at[at]
        source = lax.rem(place_ref[0] + (nz - shift), nz)
        column = place_ref[1] if sub == 0 else 1 - place_ref[1]
        lane = pl.multiple_of((source * 2 + column) * kz, kz)
        made.append(pltpu.make_async_copy(ref.at[span], x_ref.at[span, :, pl.ds(lane, kz)], sem.at[i]))
    return made


def conv_body(nz, count, plan, place_ref, *refs):
    blocks = refs[:count]
    w_refs = refs[count : count + 2]
    own_ref, first_ref, rest_ref, hot_ref, pooled_ref, mask_ref = refs[count + 2 : count + 8]
    x_ref, wv_ref, sv_ref, mv_ref, x_sem, w_sem, s_sem, m_sem = refs[count + 8 :]
    imgs, pos, kz = blocks[0].shape
    cut = imgs // 2
    depth, width = wv_ref.shape[1:]
    rows_w = w_refs[0].shape[1]
    me_y = place_ref[1]
    me_hi = place_ref[2]
    me_core = place_ref[3]
    columns = (me_y, 1 - me_y)

    def copy_x(part):
        return block_copies(nz, blocks, plan, place_ref, x_ref, x_sem.at[part], pl.ds(part * cut, cut))

    def copy_w(h):
        made = []
        for i in range(2):
            hi = me_hi if i == 0 else 1 - me_hi
            for k in range(2):
                core = me_core if k == 0 else 1 - me_core
                row = pl.multiple_of((hi * 2 + core) * rows_w, rows_w)
                made.append(
                    pltpu.make_async_copy(
                        w_refs[k].at[2 * h + i], wv_ref.at[h, pl.ds(row, rows_w)], w_sem.at[h, 2 * i + k]
                    )
                )
        return made

    copies = [copy_w(0) + copy_x(0), copy_x(1), copy_w(1)]
    edge = first_ref.shape[0]
    streams = [
        [pltpu.make_async_copy(own_ref.at[me_y], sv_ref.at[0], s_sem.at[0])],
        [
            pltpu.make_async_copy(first_ref, sv_ref.at[1, pl.ds(0, edge)], s_sem.at[1]),
            pltpu.make_async_copy(
                rest_ref.at[pl.ds(0, imgs * pos - edge)], sv_ref.at[1, pl.ds(edge, imgs * pos - edge)], s_sem.at[2]
            ),
        ],
    ]
    for c in copies[0] + streams[0] + copies[1] + copies[2] + streams[1]:
        c.start()
    pooled_ref[:, :, imgs:] = hot_ref[...]
    sends = []

    def product(h, part):
        for c in copies[part] if h == 0 else copies[2] if part == 0 else []:
            c.wait()
        x = x_ref[part * cut : (part + 1) * cut].reshape(cut * pos, depth)
        if part == 0:
            for c in streams[h]:
                c.wait()
        return jnp.dot(x, wv_ref[h], preferred_element_type=jnp.float32)

    def finish(h, part, y):
        y = (y + sv_ref[h, part * cut * pos : (part + 1) * cut * pos].astype(jnp.float32)).reshape(cut, pos, width)
        pooled = (jnp.sum(jnp.maximum(y, 0.0), axis=1) / pos).astype(jnp.bfloat16)
        for f in range(pooled_ref.shape[0]):
            pooled_ref[f, columns[h], part * cut : (part + 1) * cut] = pooled
        mv_ref[h, part] = jnp.where(y > 0.0, 1.0, 0.0).astype(jnp.bfloat16)
        sends.append(
            pltpu.make_async_copy(
                mv_ref.at[h, part], mask_ref.at[columns[h], pl.ds(part * cut, cut)], m_sem.at[h, part]
            )
        )
        sends[-1].start()

    tiles = [(h, part) for h in range(2) for part in range(2)]
    ahead = product(*tiles[0])
    for i, tile in enumerate(tiles):
        y = ahead
        if i + 1 < len(tiles):
            ahead = product(*tiles[i + 1])
        finish(*tile, y)
    for c in sends:
        c.wait()


def conv(place, blocks, plan, weights, stream2, stream_first, stream_rest, hot, nz):
    half, pos, kz = blocks[0].shape
    fs, _, _, width = hot.shape
    depth = 2 * nz * kz
    return pl.pallas_call(
        functools.partial(conv_body, nz, len(blocks), plan),
        in_specs=[pl.BlockSpec(memory_space=pltpu.SMEM)] + [HB] * (len(blocks) + 5) + [VM],
        out_specs=[VM, HB],
        out_shape=[
            jax.ShapeDtypeStruct((fs, 2, 2 * half, width), jnp.bfloat16),
            jax.ShapeDtypeStruct((2, half, pos, width), jnp.bfloat16),
        ],
        scratch_shapes=[
            pltpu.VMEM((half, pos, depth), jnp.bfloat16),
            pltpu.VMEM((2, depth, width), jnp.bfloat16),
            pltpu.VMEM((2, half * pos, width), jnp.bfloat16),
            pltpu.VMEM((2, 2, half // 2, pos, width), jnp.bfloat16),
            pltpu.SemaphoreType.DMA((2, len(plan))),
            pltpu.SemaphoreType.DMA((2, 4)),
            pltpu.SemaphoreType.DMA((3,)),
            pltpu.SemaphoreType.DMA((2, 2)),
        ],
        compiler_params=pltpu.CompilerParams(vmem_limit_bytes=32 * 1024 * 1024),
        name="conv_pool_mask",
    )(place, *[pltpu.with_memory_space_constraint(b, pltpu.HBM) for b in (*blocks, *weights, stream2, stream_first, stream_rest)], hot)


def masked_body(nz, count, plan, place_ref, *refs):
    blocks = refs[:count]
    mask_ref, pa_ref, m_ref, x_ref, mv_ref, x_sem, m_sem = refs[count:]
    imgs, pos, depth = x_ref.shape
    ka = pa_ref.shape[0]
    width = mv_ref.shape[3]
    copies = block_copies(nz, blocks, plan, place_ref, x_ref, x_sem, pl.ds(0, imgs))
    masks = [pltpu.make_async_copy(mask_ref.at[h], mv_ref.at[h], m_sem.at[h]) for h in range(2)]
    for c in copies + masks:
        c.start()
    for c in copies:
        c.wait()
    acts = lax.dot_general(
        x_ref[...].reshape(imgs * pos, depth), pa_ref[...], NT, preferred_element_type=jnp.float32
    )
    hi = acts.astype(jnp.bfloat16)
    lo = (acts - hi.astype(jnp.float32)).astype(jnp.bfloat16)
    acts = jnp.concatenate([hi, lo], axis=1)
    for c in masks:
        c.wait()
    for h in range(2):
        for i in range(imgs):
            both = lax.dot_general(
                acts[i * pos : (i + 1) * pos, :], mv_ref[h, i], TN, preferred_element_type=jnp.float32
            )
            m_ref[i, :, h * width : (h + 1) * width] = both[:ka] + both[ka:]


def masked_sums(place, blocks, plan, mask, proj_act, nz):
    two, imgs, pos, width = mask.shape
    ka, depth = proj_act.shape
    return pl.pallas_call(
        functools.partial(masked_body, nz, len(blocks), plan),
        in_specs=[pl.BlockSpec(memory_space=pltpu.SMEM)] + [HB] * (len(blocks) + 1) + [VM],
        out_specs=VM,
        out_shape=jax.ShapeDtypeStruct((imgs, ka, two * width), jnp.float32),
        scratch_shapes=[
            pltpu.VMEM((imgs, pos, depth), jnp.bfloat16),
            pltpu.VMEM(mask.shape, jnp.bfloat16),
            pltpu.SemaphoreType.DMA((len(plan),)),
            pltpu.SemaphoreType.DMA((2,)),
        ],
        compiler_params=pltpu.CompilerParams(vmem_limit_bytes=32 * 1024 * 1024),
        name="masked_sums",
    )(place, *[pltpu.with_memory_space_constraint(b, pltpu.HBM) for b in blocks], mask, proj_act)


def logits_body(both_ref, head_ref, out_ref):
    share = out_ref.shape[2]
    some, rows, width = both_ref.shape
    pooled = both_ref[:, : rows // 2].astype(jnp.float32).reshape(some * rows // 2, width).astype(jnp.bfloat16)
    for s in range(out_ref.shape[0]):
        part = jnp.dot(pooled, head_ref[:, s * share : (s + 1) * share], preferred_element_type=jnp.float32)
        out_ref[s] = part.astype(jnp.bfloat16)


def logits_slices(both, head, n):
    some, rows, _ = both.shape
    return pl.pallas_call(
        logits_body,
        in_specs=[VM, VM],
        out_specs=VM,
        out_shape=jax.ShapeDtypeStruct((n, some * rows // 2, head.shape[1] // n), jnp.bfloat16),
        compiler_params=LIMIT,
        name="logits_slices",
    )(both, head)


def back_body(expo_ref, head_ref, out_ref, hv_ref, sem):
    depth, classes = head_ref.shape
    n, _, share = expo_ref.shape
    pieces = sem.shape[0]
    size = classes // pieces
    copies = [
        pltpu.make_async_copy(head_ref.at[:, pl.ds(p * size, size)], hv_ref.at[p], sem.at[p]) for p in range(pieces)
    ]
    for c in copies:
        c.start()
    e = jnp.concatenate([expo_ref[s] for s in range(n)], axis=1)
    total = jnp.sum(e.astype(jnp.float32), axis=1, keepdims=True)
    out_ref[:, depth:] = jnp.broadcast_to(total, (out_ref.shape[0], 128))
    acc = jnp.zeros((out_ref.shape[0], depth), jnp.float32)
    for p in range(pieces):
        copies[p].wait()
        acc += lax.dot_general(
            e[:, p * size : (p + 1) * size], hv_ref[p], NT, preferred_element_type=jnp.float32
        )
    out_ref[:, :depth] = acc


def back(expo, head):
    rows = expo.shape[1]
    depth, classes = head.shape
    pieces = 4
    return pl.pallas_call(
        back_body,
        in_specs=[VM, HB],
        out_specs=VM,
        out_shape=jax.ShapeDtypeStruct((rows, depth + 128), jnp.float32),
        scratch_shapes=[
            pltpu.VMEM((pieces, depth, classes // pieces), head.dtype),
            pltpu.SemaphoreType.DMA((pieces,)),
        ],
        compiler_params=LIMIT,
        name="back",
    )(expo, pltpu.with_memory_space_constraint(head, pltpu.HBM))


def final_body(pos, place_ref, m_ref, part_ref, hot_ref, own_ref, other_ref, out_ref):
    width = hot_ref.shape[3]
    imgs, ka, _ = m_ref.shape
    acc = jnp.zeros(out_ref.shape, jnp.float32)
    for k, pe_ref in enumerate((own_ref, other_ref)):
        h = place_ref[1] if k == 0 else 1 - place_ref[1]
        part = sum(part_ref[a, h] for a in range(part_ref.shape[0]))
        hot = sum(hot_ref[a, h].astype(jnp.float32)[imgs:] for a in range(hot_ref.shape[0]))
        d = part[:, :width] / part[:, width : width + 1] - hot
        d = (d / pos).astype(jnp.bfloat16).astype(jnp.float32)
        lane = pl.multiple_of(h * width, width)
        v = (m_ref[:, :, pl.ds(lane, width)] * d[:, None, :]).reshape(imgs * ka, width)
        v_hi = v.astype(jnp.bfloat16)
        v_lo = (v - v_hi.astype(jnp.float32)).astype(jnp.bfloat16)
        acc += lax.dot_general(v_hi, pe_ref[...], NT, preferred_element_type=jnp.float32)
        acc += lax.dot_general(v_lo, pe_ref[...], NT, preferred_element_type=jnp.float32)
    out_ref[...] = acc


def final(place, m, part, hot, pe_own, pe_other, pos):
    imgs, ka, _ = m.shape
    return pl.pallas_call(
        functools.partial(final_body, pos),
        in_specs=[pl.BlockSpec(memory_space=pltpu.SMEM)] + [VM] * 5,
        out_specs=VM,
        out_shape=jax.ShapeDtypeStruct((imgs * ka, pe_own.shape[0]), jnp.float32),
        compiler_params=LIMIT,
        name="final",
    )(place, m, part, hot, pe_own, pe_other)


def per_device(stream, mid, conv_weight, head_weight, labels, proj_act, proj_err):
    images, pos, width = stream.shape
    kz = mid.shape[2]
    half = images // 2
    nz = lax.axis_size("z")
    parts = nz * 2
    fs = lax.axis_size("yhi") * lax.axis_size("core")
    block = head_weight.shape[1]
    me_y = lax.axis_index("ylo")
    f = lax.axis_index("yhi") * lax.axis_size("core") + lax.axis_index("core")
    swap = [(0, 1), (1, 0)]

    mid = mid.reshape(2, half, pos, kz)
    stream = stream.reshape(2, half, pos, width)
    mine = lax.dynamic_index_in_dim(mid, me_y, 0, keepdims=False)
    theirs = lax.dynamic_index_in_dim(mid, 1 - me_y, 0, keepdims=False)
    swapped = lax.ppermute(theirs, "ylo", swap)
    pe_own = proj_err.T
    sent = lax.dynamic_index_in_dim(stream, 1 - me_y, 0, keepdims=False).reshape(half * pos, width)
    cut = (half * pos + pe_own.shape[0]) // 2
    stream_first = lax.ppermute(sent[:cut], "ylo", swap)
    stream_rest = lax.ppermute(jnp.concatenate([sent[cut:], pe_own], axis=0), "ylo", swap)
    blocks, weights, plan = rings(mine, swapped, nz, conv_weight, stream_first)

    classes = f * block + jnp.arange(block, dtype=jnp.int32)
    onehot = (labels[:, None] == classes[None, :]).astype(jnp.bfloat16)
    hot = lax.dot_general(onehot, head_weight, NT, preferred_element_type=jnp.float32)
    hot = hot.astype(jnp.bfloat16).reshape(fs, 2, half, width)

    blocks, weights, stream_rest, hot = lax.optimization_barrier((blocks, weights, stream_rest, hot))
    place = jnp.stack([lax.axis_index(a) for a in ("z", "ylo", "yhi", "core")]).astype(jnp.int32)
    both, mask = conv(
        place, blocks, plan, weights,
        stream.reshape(2, half * pos, width), stream_first, stream_rest, hot, nz,
    )

    both = lax.all_to_all(both.reshape(2 * fs, 2 * half, width), ROWS, 0, 0)
    part = lax.all_to_all(logits_slices(both, head_weight, parts), SPREAD, 0, 0)
    mask, both = lax.optimization_barrier((mask, both))
    m = masked_sums(place, blocks, plan, mask, proj_act.T, nz)
    pe_other = stream_rest[half * pos - cut :]
    part, m, pe_other = lax.optimization_barrier((part, m, pe_other))

    logits = jnp.sum(part.astype(jnp.float32), axis=0)
    expo = jnp.minimum(jnp.exp(logits), BF16_TOP).astype(jnp.bfloat16)
    expo = lax.all_to_all(jnp.broadcast_to(expo, (parts,) + expo.shape), SPREAD, 0, 0)

    part = back(expo, head_weight).reshape(2 * fs, half, width + 128)
    part = lax.all_to_all(part, ROWS, 0, 0).reshape(fs, 2, half, width + 128)

    grads = final(place, m, part, both.reshape(fs, 2, 2 * half, width), pe_own, pe_other, pos)
    grads = grads.reshape(half, nz, 2, -1).transpose(2, 1, 0, 3).reshape(parts, half, -1)
    grads = lax.all_to_all(grads, SPREAD, 0, 0)
    grads = jnp.sum(grads.reshape(2, nz, half, -1), axis=1)
    return grads.reshape(images, -1)


def solution(mesh):
    fine = Mesh(mesh.devices.reshape(4, 8, 2, 2, 2), ("seed", "z", "ylo", "yhi", "core"))
    rows = ("seed", "yhi", "core")
    in_specs = (
        P(rows, None, CHAN),
        P(rows, None, CHAN),
        P(rows, CHAN),
        P(("seed", "z", "ylo"), ("yhi", "core")),
        P(),
        P(),
        P(CHAN, None),
    )
    return jax.shard_map(
        per_device, mesh=fine, in_specs=in_specs, out_specs=P(rows, CHAN), check_vma=False
    )
```

```python
import functools

import jax
import jax.numpy as jnp
from jax import lax
from jax.experimental import pallas as pl
from jax.experimental.pallas import tpu as pltpu
from jax.sharding import Mesh, PartitionSpec as P

CHAN = ("z", "ylo")
SPREAD = ("ylo", "z")
ROWS = ("yhi", "core", "ylo")
BF16_TOP = 3.3895313892515355e38
NT = (((1,), (1,)), ((), ()))
TN = (((0,), (0,)), ((), ()))
VM = pl.BlockSpec(memory_space=pltpu.VMEM)
HB = pl.BlockSpec(memory_space=pltpu.HBM)
LIMIT = pltpu.CompilerParams(vmem_limit_bytes=16 * 1024 * 1024)


def rings(mine, swapped, nz, w, early, hot):
    right = [(i, (i + 1) % nz) for i in range(nz)]
    left = [(i, (i - 1) % nz) for i in range(nz)]
    r = lax.ppermute(mine, "z", right)
    l = lax.ppermute(mine, "z", left)
    r, l, swapped, w = lax.optimization_barrier((r, l, swapped, w))
    swap = [(0, 1), (1, 0)]
    across = [(i, 3 - i) for i in range(4)]
    low = lax.ppermute(w, "ylo", swap)
    high = lax.ppermute(w, ("ylo", "yhi"), across)
    arrays = [mine, swapped, r, l]
    plan = [(0, None, 0, 0), (1, None, 1, 0), (2, None, 0, 1), (3, None, 0, nz - 1)]
    r = jnp.stack([r, swapped])
    l = jnp.stack([l, swapped])
    for k in range(2, nz // 2):
        r = lax.ppermute(r, "z", right)
        l = lax.ppermute(l, "z", left)
        if k == 2:
            r, l = lax.optimization_barrier((r, l))
            low, high, *_ = lax.optimization_barrier((low, high, r, l))
            far = lax.ppermute(low, ("ylo", "yhi"), across)
        elif k == nz // 2 - 1:
            r, l, far, early, hot = lax.optimization_barrier((r, l, far, early, hot))
            every = jnp.stack([w, far, low, high])
            weights = [every, lax.ppermute(every, "core", swap)]
        for way, v in ((1, r), (-1, l)):
            plan += [(len(arrays), 0, 0, way * k % nz), (len(arrays), 1, 1, way * (k - 1) % nz)]
            arrays.append(v)
    last = nz // 2
    r = lax.ppermute(r, "z", right)
    plan += [(len(arrays), 0, 0, last), (len(arrays), 1, 1, last - 1)]
    arrays.append(r)
    l = l[1]
    for k in (last + 1, last):
        l = lax.ppermute(l, "z", left)
        plan.append((len(arrays), None, 1, k))
        arrays.append(l)
    return arrays, weights, hot, tuple(plan)


def in_hbm(arrays):
    return [pltpu.with_memory_space_constraint(a, pltpu.HBM) for a in arrays]


def block_copies(nz, blocks, plan, place_ref, x_ref, sem, span, relative):
    kz = blocks[0].shape[2]
    made = []
    for i, (array, at, sub, shift) in enumerate(plan):
        ref = blocks[array] if at is None else blocks[array].at[at]
        source = lax.rem(place_ref[0] + (nz - shift), nz)
        column = place_ref[1] if sub == 0 else 1 - place_ref[1]
        if relative:
            hi = source // 4
            core = lax.rem(source // 2, 2)
            source = 4 * jnp.abs(hi - place_ref[2]) + 2 * jnp.abs(core - place_ref[3]) + lax.rem(source, 2)
        lane = pl.multiple_of((source * 2 + column) * kz, kz)
        made.append(pltpu.make_async_copy(ref.at[span], x_ref.at[span, :, pl.ds(lane, kz)], sem.at[i]))
    return made


def conv_body(nz, count, plan, place_ref, *refs):
    blocks = refs[:count]
    w_refs = refs[count : count + 2]
    own_ref, first_ref, rest_ref, hot_ref, pooled_ref, mask_ref = refs[count + 2 : count + 8]
    x_ref, sv_ref, mv_ref, x_sem, s_sem, m_sem = refs[count + 8 :]
    imgs, pos, kz = blocks[0].shape
    cut = imgs // 2
    depth = x_ref.shape[2]
    width = sv_ref.shape[2]
    me_y = place_ref[1]
    columns = (me_y, 1 - me_y)

    def copy_x(part):
        return block_copies(nz, blocks, plan, place_ref, x_ref, x_sem.at[part], pl.ds(part * cut, cut), True)

    copies = [copy_x(0), copy_x(1)]
    edge = first_ref.shape[0]
    streams = [
        [pltpu.make_async_copy(own_ref.at[me_y], sv_ref.at[0], s_sem.at[0])],
        [
            pltpu.make_async_copy(first_ref, sv_ref.at[1, pl.ds(0, edge)], s_sem.at[1]),
            pltpu.make_async_copy(
                rest_ref.at[pl.ds(0, imgs * pos - edge)], sv_ref.at[1, pl.ds(edge, imgs * pos - edge)], s_sem.at[2]
            ),
        ],
    ]
    for c in copies[0] + streams[0] + copies[1] + streams[1]:
        c.start()
    pooled_ref[:, :, imgs:] = hot_ref[...]
    sends = []

    def product(h, part):
        for c in copies[part] if h == 0 else []:
            c.wait()
        x = x_ref[part * cut : (part + 1) * cut].reshape(cut * pos, depth)
        if part == 0:
            for c in streams[h]:
                c.wait()
        w = jnp.concatenate([w_refs[k][2 * h + i] for i in range(2) for k in range(2)], axis=0)
        return jnp.dot(x, w, preferred_element_type=jnp.float32)

    def finish(h, part, y):
        y = (y + sv_ref[h, part * cut * pos : (part + 1) * cut * pos].astype(jnp.float32)).reshape(cut, pos, width)
        pooled = (jnp.sum(jnp.maximum(y, 0.0), axis=1) / pos).astype(jnp.bfloat16)
        for f in range(pooled_ref.shape[0]):
            pooled_ref[f, columns[h], part * cut : (part + 1) * cut] = pooled
        mv_ref[h, part] = jnp.where(y > 0.0, 1.0, 0.0).astype(jnp.bfloat16)
        sends.append(
            pltpu.make_async_copy(
                mv_ref.at[h, part], mask_ref.at[columns[h], pl.ds(part * cut, cut)], m_sem.at[h, part]
            )
        )
        sends[-1].start()

    tiles = [(h, part) for h in range(2) for part in range(2)]
    ahead = product(*tiles[0])
    for i, tile in enumerate(tiles):
        y = ahead
        if i + 1 < len(tiles):
            ahead = product(*tiles[i + 1])
        finish(*tile, y)
    for c in sends:
        c.wait()


def conv(place, blocks, plan, weights, stream2, stream_first, stream_rest, hot, nz):
    half, pos, kz = blocks[0].shape
    fs, _, _, width = hot.shape
    depth = 2 * nz * kz
    return pl.pallas_call(
        functools.partial(conv_body, nz, len(blocks), plan),
        in_specs=[pl.BlockSpec(memory_space=pltpu.SMEM)] + [HB] * len(blocks) + [VM, VM] + [HB] * 3 + [VM],
        out_specs=[VM, HB],
        out_shape=[
            jax.ShapeDtypeStruct((fs, 2, 2 * half, width), jnp.bfloat16),
            jax.ShapeDtypeStruct((2, half, pos, width), jnp.bfloat16),
        ],
        scratch_shapes=[
            pltpu.VMEM((half, pos, depth), jnp.bfloat16),
            pltpu.VMEM((2, half * pos, width), jnp.bfloat16),
            pltpu.VMEM((2, 2, half // 2, pos, width), jnp.bfloat16),
            pltpu.SemaphoreType.DMA((2, len(plan))),
            pltpu.SemaphoreType.DMA((3,)),
            pltpu.SemaphoreType.DMA((2, 2)),
        ],
        compiler_params=pltpu.CompilerParams(vmem_limit_bytes=50 * 1024 * 1024),
        name="conv_pool_mask",
    )(place, *in_hbm(blocks), *weights, *in_hbm((stream2, stream_first, stream_rest)), hot)


def masked_body(nz, count, plan, place_ref, *refs):
    blocks = refs[:count]
    mask_ref, pa_ref, m_ref, x_ref, mv_ref, x_sem, m_sem = refs[count:]
    imgs, pos, depth = x_ref.shape
    ka = pa_ref.shape[0]
    width = mv_ref.shape[3]
    copies = block_copies(nz, blocks, plan, place_ref, x_ref, x_sem, pl.ds(0, imgs), False)
    masks = [pltpu.make_async_copy(mask_ref.at[h], mv_ref.at[h], m_sem.at[h]) for h in range(2)]
    for c in copies + masks:
        c.start()
    for c in copies:
        c.wait()
    acts = lax.dot_general(
        x_ref[...].reshape(imgs * pos, depth), pa_ref[...], NT, preferred_element_type=jnp.float32
    )
    hi = acts.astype(jnp.bfloat16)
    lo = (acts - hi.astype(jnp.float32)).astype(jnp.bfloat16)
    acts = jnp.concatenate([hi, lo], axis=1)
    for c in masks:
        c.wait()
    for h in range(2):
        for i in range(imgs):
            both = lax.dot_general(
                acts[i * pos : (i + 1) * pos, :], mv_ref[h, i], TN, preferred_element_type=jnp.float32
            )
            m_ref[i, :, h * width : (h + 1) * width] = both[:ka] + both[ka:]


def masked_sums(place, blocks, plan, mask, proj_act, nz):
    two, imgs, pos, width = mask.shape
    ka, depth = proj_act.shape
    return pl.pallas_call(
        functools.partial(masked_body, nz, len(blocks), plan),
        in_specs=[pl.BlockSpec(memory_space=pltpu.SMEM)] + [HB] * (len(blocks) + 1) + [VM],
        out_specs=VM,
        out_shape=jax.ShapeDtypeStruct((imgs, ka, two * width), jnp.float32),
        scratch_shapes=[
            pltpu.VMEM((imgs, pos, depth), jnp.bfloat16),
            pltpu.VMEM(mask.shape, jnp.bfloat16),
            pltpu.SemaphoreType.DMA((len(plan),)),
            pltpu.SemaphoreType.DMA((2,)),
        ],
        compiler_params=pltpu.CompilerParams(vmem_limit_bytes=32 * 1024 * 1024),
        name="masked_sums",
    )(place, *in_hbm(blocks), mask, proj_act)


def logits_body(both_ref, head_ref, out_ref):
    share = out_ref.shape[2]
    some, rows, width = both_ref.shape
    pooled = both_ref[:, : rows // 2].astype(jnp.float32).reshape(some * rows // 2, width).astype(jnp.bfloat16)
    for s in range(out_ref.shape[0]):
        part = jnp.dot(pooled, head_ref[:, s * share : (s + 1) * share], preferred_element_type=jnp.float32)
        out_ref[s] = part.astype(jnp.bfloat16)


def logits_slices(both, head, n):
    some, rows, _ = both.shape
    return pl.pallas_call(
        logits_body,
        in_specs=[VM, VM],
        out_specs=VM,
        out_shape=jax.ShapeDtypeStruct((n, some * rows // 2, head.shape[1] // n), jnp.bfloat16),
        compiler_params=LIMIT,
        name="logits_slices",
    )(both, head)


def back_body(expo_ref, head_ref, out_ref, hv_ref, sem):
    depth, classes = head_ref.shape
    n, _, share = expo_ref.shape
    pieces = sem.shape[0]
    size = classes // pieces
    copies = [
        pltpu.make_async_copy(head_ref.at[:, pl.ds(p * size, size)], hv_ref.at[p], sem.at[p]) for p in range(pieces)
    ]
    for c in copies:
        c.start()
    e = jnp.concatenate([expo_ref[s] for s in range(n)], axis=1)
    total = jnp.sum(e.astype(jnp.float32), axis=1, keepdims=True)
    out_ref[:, depth:] = jnp.broadcast_to(total, (out_ref.shape[0], 128))
    acc = jnp.zeros((out_ref.shape[0], depth), jnp.float32)
    for p in range(pieces):
        copies[p].wait()
        acc += lax.dot_general(
            e[:, p * size : (p + 1) * size], hv_ref[p], NT, preferred_element_type=jnp.float32
        )
    out_ref[:, :depth] = acc


def back(expo, head):
    rows = expo.shape[1]
    depth, classes = head.shape
    pieces = 4
    return pl.pallas_call(
        back_body,
        in_specs=[VM, HB],
        out_specs=VM,
        out_shape=jax.ShapeDtypeStruct((rows, depth + 128), jnp.float32),
        scratch_shapes=[
            pltpu.VMEM((pieces, depth, classes // pieces), head.dtype),
            pltpu.SemaphoreType.DMA((pieces,)),
        ],
        compiler_params=LIMIT,
        name="back",
    )(expo, pltpu.with_memory_space_constraint(head, pltpu.HBM))


def final_body(pos, place_ref, m_ref, part_ref, hot_ref, own_ref, other_ref, out_ref):
    width = hot_ref.shape[3]
    imgs, ka, _ = m_ref.shape
    acc = jnp.zeros(out_ref.shape, jnp.float32)
    for k, pe_ref in enumerate((own_ref, other_ref)):
        h = place_ref[1] if k == 0 else 1 - place_ref[1]
        part = sum(part_ref[a, h] for a in range(part_ref.shape[0]))
        hot = sum(hot_ref[a, h].astype(jnp.float32)[imgs:] for a in range(hot_ref.shape[0]))
        d = part[:, :width] / part[:, width : width + 1] - hot
        d = (d / pos).astype(jnp.bfloat16).astype(jnp.float32)
        lane = pl.multiple_of(h * width, width)
        v = (m_ref[:, :, pl.ds(lane, width)] * d[:, None, :]).reshape(imgs * ka, width)
        v_hi = v.astype(jnp.bfloat16)
        v_lo = (v - v_hi.astype(jnp.float32)).astype(jnp.bfloat16)
        acc += lax.dot_general(v_hi, pe_ref[...], NT, preferred_element_type=jnp.float32)
        acc += lax.dot_general(v_lo, pe_ref[...], NT, preferred_element_type=jnp.float32)
    out_ref[...] = acc


def final(place, m, part, hot, pe_own, pe_other, pos):
    imgs, ka, _ = m.shape
    return pl.pallas_call(
        functools.partial(final_body, pos),
        in_specs=[pl.BlockSpec(memory_space=pltpu.SMEM)] + [VM] * 5,
        out_specs=VM,
        out_shape=jax.ShapeDtypeStruct((imgs * ka, pe_own.shape[0]), jnp.float32),
        compiler_params=LIMIT,
        name="final",
    )(place, m, part, hot, pe_own, pe_other)


def per_device(stream, mid, conv_weight, head_weight, labels, proj_act, proj_err):
    images, pos, width = stream.shape
    kz = mid.shape[2]
    half = images // 2
    nz = lax.axis_size("z")
    parts = nz * 2
    fs = lax.axis_size("yhi") * lax.axis_size("core")
    block = head_weight.shape[1]
    me_y = lax.axis_index("ylo")
    f = lax.axis_index("yhi") * lax.axis_size("core") + lax.axis_index("core")
    swap = [(0, 1), (1, 0)]

    mid = mid.reshape(2, half, pos, kz)
    stream = stream.reshape(2, half, pos, width)
    mine = lax.dynamic_index_in_dim(mid, me_y, 0, keepdims=False)
    theirs = lax.dynamic_index_in_dim(mid, 1 - me_y, 0, keepdims=False)
    swapped = lax.ppermute(theirs, "ylo", swap)
    pe_own = proj_err.T
    sent = lax.dynamic_index_in_dim(stream, 1 - me_y, 0, keepdims=False).reshape(half * pos, width)
    cut = (half * pos + pe_own.shape[0]) // 2
    stream_first = lax.ppermute(sent[:cut], "ylo", swap)
    stream_rest = lax.ppermute(jnp.concatenate([sent[cut:], pe_own], axis=0), "ylo", swap)
    classes = f * block + jnp.arange(block, dtype=jnp.int32)
    onehot = (labels[:, None] == classes[None, :]).astype(jnp.bfloat16)
    hot = lax.dot_general(onehot, head_weight, NT, preferred_element_type=jnp.float32)
    hot = hot.astype(jnp.bfloat16).reshape(fs, 2, half, width)
    blocks, weights, hot, plan = rings(mine, swapped, nz, conv_weight, stream_first, hot)


    blocks, weights, stream_rest, hot = lax.optimization_barrier((blocks, weights, stream_rest, hot))
    place = jnp.stack([lax.axis_index(a) for a in ("z", "ylo", "yhi", "core")]).astype(jnp.int32)
    both, mask = conv(
        place, blocks, plan, weights,
        stream.reshape(2, half * pos, width), stream_first, stream_rest, hot, nz,
    )

    both = lax.all_to_all(both.reshape(2 * fs, 2 * half, width), ROWS, 0, 0)
    part = lax.all_to_all(logits_slices(both, head_weight, parts), SPREAD, 0, 0)
    mask, both = lax.optimization_barrier((mask, both))
    m = masked_sums(place, blocks, plan, mask, proj_act.T, nz)
    pe_other = stream_rest[half * pos - cut :]
    part, m, pe_other = lax.optimization_barrier((part, m, pe_other))

    logits = jnp.sum(part.astype(jnp.float32), axis=0)
    expo = jnp.minimum(jnp.exp(logits), BF16_TOP).astype(jnp.bfloat16)
    expo = lax.all_to_all(jnp.broadcast_to(expo, (parts,) + expo.shape), SPREAD, 0, 0)

    part = back(expo, head_weight).reshape(2 * fs, half, width + 128)
    part = lax.all_to_all(part, ROWS, 0, 0).reshape(fs, 2, half, width + 128)

    grads = final(place, m, part, both.reshape(fs, 2, 2 * half, width), pe_own, pe_other, pos)
    grads = grads.reshape(half, nz, 2, -1).transpose(2, 1, 0, 3).reshape(parts, half, -1)
    grads = lax.all_to_all(grads, SPREAD, 0, 0)
    grads = jnp.sum(grads.reshape(2, nz, half, -1), axis=1)
    return grads.reshape(images, -1)


def solution(mesh):
    fine = Mesh(mesh.devices.reshape(4, 8, 2, 2, 2), ("seed", "z", "ylo", "yhi", "core"))
    rows = ("seed", "yhi", "core")
    in_specs = (
        P(rows, None, CHAN),
        P(rows, None, CHAN),
        P(rows, CHAN),
        P(("seed", "z", "ylo"), ("yhi", "core")),
        P(),
        P(),
        P(CHAN, None),
    )
    return jax.shard_map(
        per_device, mesh=fine, in_specs=in_specs, out_specs=P(rows, CHAN), check_vma=False
    )
```

```python
import functools

import jax
import jax.numpy as jnp
from jax import lax
from jax.experimental import pallas as pl
from jax.experimental.pallas import tpu as pltpu
from jax.sharding import Mesh, PartitionSpec as P

CHAN = ("z", "ylo")
SPREAD = ("ylo", "z")
ROWS = ("yhi", "core", "ylo")
BF16_TOP = 3.3895313892515355e38
NT = (((1,), (1,)), ((), ()))
TN = (((0,), (0,)), ((), ()))
VM = pl.BlockSpec(memory_space=pltpu.VMEM)
HB = pl.BlockSpec(memory_space=pltpu.HBM)
LIMIT = pltpu.CompilerParams(vmem_limit_bytes=16 * 1024 * 1024)


def rings(mine, swapped, nz, w, early):
    right = [(i, (i + 1) % nz) for i in range(nz)]
    left = [(i, (i - 1) % nz) for i in range(nz)]
    r = lax.ppermute(mine, "z", right)
    l = lax.ppermute(mine, "z", left)
    r, l, swapped, w = lax.optimization_barrier((r, l, swapped, w))
    swap = [(0, 1), (1, 0)]
    across = [(i, 3 - i) for i in range(4)]
    low = lax.ppermute(w, "ylo", swap)
    high = lax.ppermute(w, ("ylo", "yhi"), across)
    arrays = [mine, swapped, r, l]
    plan = [(0, None, 0, 0), (1, None, 1, 0), (2, None, 0, 1), (3, None, 0, nz - 1)]
    r = jnp.stack([r, swapped])
    l = jnp.stack([l, swapped])
    for k in range(2, nz // 2):
        end = k == nz // 2 - 1
        r = lax.ppermute(r, "z", right)
        if end:
            follow = lax.ppermute(l[1], "z", left)
            l = lax.ppermute(l[0], "z", left)
        else:
            l = lax.ppermute(l, "z", left)
        if k == 2:
            r, l = lax.optimization_barrier((r, l))
            low, high, *_ = lax.optimization_barrier((low, high, r, l))
            far = lax.ppermute(low, ("ylo", "yhi"), across)
        if end:
            r, l, follow, far, early = lax.optimization_barrier((r, l, follow, far, early))
            every = jnp.stack([w, far, low, high])
            weights = [every, lax.ppermute(every, "core", swap)]
        plan += [(len(arrays), 0, 0, k), (len(arrays), 1, 1, k - 1)]
        arrays.append(r)
        if end:
            plan += [(len(arrays), None, 0, nz - k), (len(arrays) + 1, None, 1, nz - k + 1)]
            arrays += [l, follow]
        else:
            plan += [(len(arrays), 0, 0, nz - k), (len(arrays), 1, 1, nz - k + 1)]
            arrays.append(l)
    last = nz // 2
    r = lax.ppermute(r, "z", right)
    plan += [(len(arrays), 0, 0, last), (len(arrays), 1, 1, last - 1)]
    arrays.append(r)
    l = follow
    for k in (last + 1, last):
        l = lax.ppermute(l, "z", left)
        plan.append((len(arrays), None, 1, k))
        arrays.append(l)
    return arrays, weights, tuple(plan)


def block_copies(nz, blocks, plan, place_ref, x_ref, sem, span):
    kz = blocks[0].shape[2]
    made = []
    for i, (array, at, sub, shift) in enumerate(plan):
        ref = blocks[array] if at is None else blocks[array].at[at]
        source = lax.rem(place_ref[0] + (nz - shift), nz)
        column = place_ref[1] if sub == 0 else 1 - place_ref[1]
        lane = pl.multiple_of((source * 2 + column) * kz, kz)
        made.append(pltpu.make_async_copy(ref.at[span], x_ref.at[span, :, pl.ds(lane, kz)], sem.at[i]))
    return made


def conv_body(nz, count, plan, place_ref, *refs):
    blocks = refs[:count]
    w_refs = refs[count : count + 2]
    own_ref, first_ref, rest_ref, hot_ref, pooled_ref, mask_ref = refs[count + 2 : count + 8]
    x_ref, wv_ref, sv_ref, mv_ref, x_sem, w_sem, s_sem, m_sem = refs[count + 8 :]
    imgs, pos, kz = blocks[0].shape
    cut = imgs // 2
    depth, width = wv_ref.shape[1:]
    rows_w = w_refs[0].shape[1]
    me_y = place_ref[1]
    me_hi = place_ref[2]
    me_core = place_ref[3]
    columns = (me_y, 1 - me_y)

    def copy_x(part):
        return block_copies(nz, blocks, plan, place_ref, x_ref, x_sem.at[part], pl.ds(part * cut, cut))

    def copy_w(h):
        made = []
        for i in range(2):
            hi = me_hi if i == 0 else 1 - me_hi
            for k in range(2):
                core = me_core if k == 0 else 1 - me_core
                row = pl.multiple_of((hi * 2 + core) * rows_w, rows_w)
                made.append(
                    pltpu.make_async_copy(
                        w_refs[k].at[2 * h + i], wv_ref.at[h, pl.ds(row, rows_w)], w_sem.at[h, 2 * i + k]
                    )
                )
        return made

    copies = [copy_w(0) + copy_x(0), copy_x(1), copy_w(1)]
    edge = first_ref.shape[0]
    streams = [
        [pltpu.make_async_copy(own_ref.at[me_y], sv_ref.at[0], s_sem.at[0])],
        [
            pltpu.make_async_copy(first_ref, sv_ref.at[1, pl.ds(0, edge)], s_sem.at[1]),
            pltpu.make_async_copy(
                rest_ref.at[pl.ds(0, imgs * pos - edge)], sv_ref.at[1, pl.ds(edge, imgs * pos - edge)], s_sem.at[2]
            ),
        ],
    ]
    for c in copies[0] + streams[0] + copies[1] + copies[2] + streams[1]:
        c.start()
    pooled_ref[:, :, imgs:] = hot_ref[...]
    sends = []

    def product(h, part):
        for c in copies[part] if h == 0 else copies[2] if part == 0 else []:
            c.wait()
        x = x_ref[part * cut : (part + 1) * cut].reshape(cut * pos, depth)
        if part == 0:
            for c in streams[h]:
                c.wait()
        return jnp.dot(x, wv_ref[h], preferred_element_type=jnp.float32)

    def finish(h, part, y):
        y = (y + sv_ref[h, part * cut * pos : (part + 1) * cut * pos].astype(jnp.float32)).reshape(cut, pos, width)
        pooled = (jnp.sum(jnp.maximum(y, 0.0), axis=1) / pos).astype(jnp.bfloat16)
        for f in range(pooled_ref.shape[0]):
            pooled_ref[f, columns[h], part * cut : (part + 1) * cut] = pooled
        mv_ref[h, part] = jnp.where(y > 0.0, 1.0, 0.0).astype(jnp.bfloat16)
        sends.append(
            pltpu.make_async_copy(
                mv_ref.at[h, part], mask_ref.at[columns[h], pl.ds(part * cut, cut)], m_sem.at[h, part]
            )
        )
        sends[-1].start()

    tiles = [(h, part) for h in range(2) for part in range(2)]
    ahead = product(*tiles[0])
    for i, tile in enumerate(tiles):
        y = ahead
        if i + 1 < len(tiles):
            ahead = product(*tiles[i + 1])
        finish(*tile, y)
    for c in sends:
        c.wait()


def conv(place, blocks, plan, weights, stream2, stream_first, stream_rest, hot, nz):
    half, pos, kz = blocks[0].shape
    fs, _, _, width = hot.shape
    depth = 2 * nz * kz
    return pl.pallas_call(
        functools.partial(conv_body, nz, len(blocks), plan),
        in_specs=[pl.BlockSpec(memory_space=pltpu.SMEM)] + [HB] * (len(blocks) + 5) + [VM],
        out_specs=[VM, HB],
        out_shape=[
            jax.ShapeDtypeStruct((fs, 2, 2 * half, width), jnp.bfloat16),
            jax.ShapeDtypeStruct((2, half, pos, width), jnp.bfloat16),
        ],
        scratch_shapes=[
            pltpu.VMEM((half, pos, depth), jnp.bfloat16),
            pltpu.VMEM((2, depth, width), jnp.bfloat16),
            pltpu.VMEM((2, half * pos, width), jnp.bfloat16),
            pltpu.VMEM((2, 2, half // 2, pos, width), jnp.bfloat16),
            pltpu.SemaphoreType.DMA((2, len(plan))),
            pltpu.SemaphoreType.DMA((2, 4)),
            pltpu.SemaphoreType.DMA((3,)),
            pltpu.SemaphoreType.DMA((2, 2)),
        ],
        compiler_params=pltpu.CompilerParams(vmem_limit_bytes=32 * 1024 * 1024),
        name="conv_pool_mask",
    )(place, *[pltpu.with_memory_space_constraint(b, pltpu.HBM) for b in (*blocks, *weights, stream2, stream_first, stream_rest)], hot)


def masked_body(nz, count, plan, place_ref, *refs):
    blocks = refs[:count]
    mask_ref, pa_ref, m_ref, x_ref, mv_ref, x_sem, m_sem = refs[count:]
    imgs, pos, depth = x_ref.shape
    ka = pa_ref.shape[0]
    width = mv_ref.shape[3]
    copies = block_copies(nz, blocks, plan, place_ref, x_ref, x_sem, pl.ds(0, imgs))
    masks = [pltpu.make_async_copy(mask_ref.at[h], mv_ref.at[h], m_sem.at[h]) for h in range(2)]
    for c in copies + masks:
        c.start()
    for c in copies:
        c.wait()
    acts = lax.dot_general(
        x_ref[...].reshape(imgs * pos, depth), pa_ref[...], NT, preferred_element_type=jnp.float32
    )
    hi = acts.astype(jnp.bfloat16)
    lo = (acts - hi.astype(jnp.float32)).astype(jnp.bfloat16)
    acts = jnp.concatenate([hi, lo], axis=1)
    for c in masks:
        c.wait()
    for h in range(2):
        for i in range(imgs):
            both = lax.dot_general(
                acts[i * pos : (i + 1) * pos, :], mv_ref[h, i], TN, preferred_element_type=jnp.float32
            )
            m_ref[i, :, h * width : (h + 1) * width] = both[:ka] + both[ka:]


def masked_sums(place, blocks, plan, mask, proj_act, nz):
    two, imgs, pos, width = mask.shape
    ka, depth = proj_act.shape
    return pl.pallas_call(
        functools.partial(masked_body, nz, len(blocks), plan),
        in_specs=[pl.BlockSpec(memory_space=pltpu.SMEM)] + [HB] * (len(blocks) + 1) + [VM],
        out_specs=VM,
        out_shape=jax.ShapeDtypeStruct((imgs, ka, two * width), jnp.float32),
        scratch_shapes=[
            pltpu.VMEM((imgs, pos, depth), jnp.bfloat16),
            pltpu.VMEM(mask.shape, jnp.bfloat16),
            pltpu.SemaphoreType.DMA((len(plan),)),
            pltpu.SemaphoreType.DMA((2,)),
        ],
        compiler_params=pltpu.CompilerParams(vmem_limit_bytes=32 * 1024 * 1024),
        name="masked_sums",
    )(place, *[pltpu.with_memory_space_constraint(b, pltpu.HBM) for b in blocks], mask, proj_act)


def logits_body(both_ref, head_ref, out_ref):
    share = out_ref.shape[2]
    some, rows, width = both_ref.shape
    pooled = both_ref[:, : rows // 2].astype(jnp.float32).reshape(some * rows // 2, width).astype(jnp.bfloat16)
    for s in range(out_ref.shape[0]):
        part = jnp.dot(pooled, head_ref[:, s * share : (s + 1) * share], preferred_element_type=jnp.float32)
        out_ref[s] = part.astype(jnp.bfloat16)


def logits_slices(both, head, n):
    some, rows, _ = both.shape
    return pl.pallas_call(
        logits_body,
        in_specs=[VM, VM],
        out_specs=VM,
        out_shape=jax.ShapeDtypeStruct((n, some * rows // 2, head.shape[1] // n), jnp.bfloat16),
        compiler_params=LIMIT,
        name="logits_slices",
    )(both, head)


def back_body(expo_ref, head_ref, out_ref, hv_ref, sem):
    depth, classes = head_ref.shape
    n, _, share = expo_ref.shape
    pieces = sem.shape[0]
    size = classes // pieces
    copies = [
        pltpu.make_async_copy(head_ref.at[:, pl.ds(p * size, size)], hv_ref.at[p], sem.at[p]) for p in range(pieces)
    ]
    for c in copies:
        c.start()
    e = jnp.concatenate([expo_ref[s] for s in range(n)], axis=1)
    total = jnp.sum(e.astype(jnp.float32), axis=1, keepdims=True)
    out_ref[:, depth:] = jnp.broadcast_to(total, (out_ref.shape[0], 128))
    acc = jnp.zeros((out_ref.shape[0], depth), jnp.float32)
    for p in range(pieces):
        copies[p].wait()
        acc += lax.dot_general(
            e[:, p * size : (p + 1) * size], hv_ref[p], NT, preferred_element_type=jnp.float32
        )
    out_ref[:, :depth] = acc


def back(expo, head):
    rows = expo.shape[1]
    depth, classes = head.shape
    pieces = 4
    return pl.pallas_call(
        back_body,
        in_specs=[VM, HB],
        out_specs=VM,
        out_shape=jax.ShapeDtypeStruct((rows, depth + 128), jnp.float32),
        scratch_shapes=[
            pltpu.VMEM((pieces, depth, classes // pieces), head.dtype),
            pltpu.SemaphoreType.DMA((pieces,)),
        ],
        compiler_params=LIMIT,
        name="back",
    )(expo, pltpu.with_memory_space_constraint(head, pltpu.HBM))


def final_body(pos, place_ref, m_ref, part_ref, hot_ref, own_ref, other_ref, out_ref):
    width = hot_ref.shape[3]
    imgs, ka, _ = m_ref.shape
    acc = jnp.zeros(out_ref.shape, jnp.float32)
    for k, pe_ref in enumerate((own_ref, other_ref)):
        h = place_ref[1] if k == 0 else 1 - place_ref[1]
        part = sum(part_ref[a, h] for a in range(part_ref.shape[0]))
        hot = sum(hot_ref[a, h].astype(jnp.float32)[imgs:] for a in range(hot_ref.shape[0]))
        d = part[:, :width] / part[:, width : width + 1] - hot
        d = (d / pos).astype(jnp.bfloat16).astype(jnp.float32)
        lane = pl.multiple_of(h * width, width)
        v = (m_ref[:, :, pl.ds(lane, width)] * d[:, None, :]).reshape(imgs * ka, width)
        v_hi = v.astype(jnp.bfloat16)
        v_lo = (v - v_hi.astype(jnp.float32)).astype(jnp.bfloat16)
        acc += lax.dot_general(v_hi, pe_ref[...], NT, preferred_element_type=jnp.float32)
        acc += lax.dot_general(v_lo, pe_ref[...], NT, preferred_element_type=jnp.float32)
    out_ref[...] = acc


def final(place, m, part, hot, pe_own, pe_other, pos):
    imgs, ka, _ = m.shape
    return pl.pallas_call(
        functools.partial(final_body, pos),
        in_specs=[pl.BlockSpec(memory_space=pltpu.SMEM)] + [VM] * 5,
        out_specs=VM,
        out_shape=jax.ShapeDtypeStruct((imgs * ka, pe_own.shape[0]), jnp.float32),
        compiler_params=LIMIT,
        name="final",
    )(place, m, part, hot, pe_own, pe_other)


def per_device(stream, mid, conv_weight, head_weight, labels, proj_act, proj_err):
    images, pos, width = stream.shape
    kz = mid.shape[2]
    half = images // 2
    nz = lax.axis_size("z")
    parts = nz * 2
    fs = lax.axis_size("yhi") * lax.axis_size("core")
    block = head_weight.shape[1]
    me_y = lax.axis_index("ylo")
    f = lax.axis_index("yhi") * lax.axis_size("core") + lax.axis_index("core")
    swap = [(0, 1), (1, 0)]

    mid = mid.reshape(2, half, pos, kz)
    stream = stream.reshape(2, half, pos, width)
    mine = lax.dynamic_index_in_dim(mid, me_y, 0, keepdims=False)
    theirs = lax.dynamic_index_in_dim(mid, 1 - me_y, 0, keepdims=False)
    swapped = lax.ppermute(theirs, "ylo", swap)
    pe_own = proj_err.T
    sent = lax.dynamic_index_in_dim(stream, 1 - me_y, 0, keepdims=False).reshape(half * pos, width)
    cut = (half * pos + pe_own.shape[0]) // 2
    stream_first = lax.ppermute(sent[:cut], "ylo", swap)
    stream_rest = lax.ppermute(jnp.concatenate([sent[cut:], pe_own], axis=0), "ylo", swap)
    blocks, weights, plan = rings(mine, swapped, nz, conv_weight, stream_first)

    classes = f * block + jnp.arange(block, dtype=jnp.int32)
    onehot = (labels[:, None] == classes[None, :]).astype(jnp.bfloat16)
    hot = lax.dot_general(onehot, head_weight, NT, preferred_element_type=jnp.float32)
    hot = hot.astype(jnp.bfloat16).reshape(fs, 2, half, width)

    blocks, weights, stream_rest, hot = lax.optimization_barrier((blocks, weights, stream_rest, hot))
    place = jnp.stack([lax.axis_index(a) for a in ("z", "ylo", "yhi", "core")]).astype(jnp.int32)
    both, mask = conv(
        place, blocks, plan, weights,
        stream.reshape(2, half * pos, width), stream_first, stream_rest, hot, nz,
    )

    both = lax.all_to_all(both.reshape(2 * fs, 2 * half, width), ROWS, 0, 0)
    part = lax.all_to_all(logits_slices(both, head_weight, parts), SPREAD, 0, 0)
    mask, both = lax.optimization_barrier((mask, both))
    m = masked_sums(place, blocks, plan, mask, proj_act.T, nz)
    pe_other = stream_rest[half * pos - cut :]
    part, m, pe_other = lax.optimization_barrier((part, m, pe_other))

    logits = jnp.sum(part.astype(jnp.float32), axis=0)
    expo = jnp.minimum(jnp.exp(logits), BF16_TOP).astype(jnp.bfloat16)
    expo = lax.all_to_all(jnp.broadcast_to(expo, (parts,) + expo.shape), SPREAD, 0, 0)

    part = back(expo, head_weight).reshape(2 * fs, half, width + 128)
    part = lax.all_to_all(part, ROWS, 0, 0).reshape(fs, 2, half, width + 128)

    grads = final(place, m, part, both.reshape(fs, 2, 2 * half, width), pe_own, pe_other, pos)
    grads = grads.reshape(half, nz, 2, -1).transpose(2, 1, 0, 3).reshape(parts, half, -1)
    grads = lax.all_to_all(grads, SPREAD, 0, 0)
    grads = jnp.sum(grads.reshape(2, nz, half, -1), axis=1)
    return grads.reshape(images, -1)


def solution(mesh):
    fine = Mesh(mesh.devices.reshape(4, 8, 2, 2, 2), ("seed", "z", "ylo", "yhi", "core"))
    rows = ("seed", "yhi", "core")
    in_specs = (
        P(rows, None, CHAN),
        P(rows, None, CHAN),
        P(rows, CHAN),
        P(("seed", "z", "ylo"), ("yhi", "core")),
        P(),
        P(),
        P(CHAN, None),
    )
    return jax.shard_map(
        per_device, mesh=fine, in_specs=in_specs, out_specs=P(rows, CHAN), check_vma=False
    )
```
